256 devices in a mesh: tm: 8 (over y, x_lo), lon: 32 (over x_hi, z, core).
Axes of the slice: x: 4 (x_hi: 2, x_lo: 2; x = x_hi * 2 + x_lo), y: 4, z: 8, core: 2. Of those that a mesh axis runs over, the one named last changes fastest.
Arguments:
- first_guess: float32 [16, 256, 80, 64], P('tm', 'lon'), may hold values from -6 to 6
- background: float32 [256, 80, 64], P('lon'), may hold values from -6 to 6
- opening_kernel_matrix: bfloat16 [256, 720], replicated, may hold values from -0.21875 to 0.21875
- hidden_layer_shift: float32 [256], replicated, may hold values from -3 to 3
- closing_kernel_matrix: bfloat16 [80, 2304], replicated, may hold values from -0.125 to 0.125
- output_layer_shift: float32 [80], replicated, may hold values from -2 to 2
- model_weight: float32 [80], replicated, may hold values from 0.5 to 2
- background_weight: float32 [80], replicated, may hold values from 0.5 to 2
- obs_cell: int32 [16, 8192], P('tm', 'lon'), may hold values from 0 to 511
- obs_chan: int32 [16, 8192], P('tm', 'lon'), may hold values from 0 to 79
- obs_value: float32 [16, 8192], P('tm', 'lon'), may hold values from -6 to 6
- obs_weight: float32 [16, 8192], P('tm', 'lon'), may hold values from 0.5 to 4
- step_size: float32 [], replicated, may hold values from 0.3 to 0.6
Outputs:
- analysis: float32 [16, 256, 80, 64], P('tm', 'lon')
- costs: float32 [2], replicated
The draws below stay inside these ranges and needn't reach their ends.
Inputs may be any that keep to these rules, and one draw needn't show every extreme that they name: `obs_cell`: the band of an observation is its column block of 256; the value counts cells of that band, longitude-major.
All inputs are finite; a program needn't handle non-finite values.
Results may differ from the reference program's by a relative error of at most 0.0085.
Values may be sent and summed in bfloat16 or wider, within the bound.
No kernel may reach another device: no remote copies, remote signals or barrier semaphores. Data moves between devices by JAX's collectives and lax.ppermute only.
A program may use at most 64 MiB of HBM per device.

```python
import math
import jax
import jax.numpy as jnp
from jax import lax

C = 80
FEAT = 256
LAT = 64
LON_DEV = 8
OBS_DEV = 256
ITERS = 2
NSUB = 16
NLON = 256
OBS = 8192


def set_ends(result, rng, smallest, largest):
    longest = result.shape.index(max(result.shape))
    spots = []
    for shift in (0, 1):
        where = [jax.random.randint(jax.random.fold_in(rng, axis), (), 0, length) for axis, length in enumerate(result.shape)]
        where[longest] = (where[longest] + shift) % result.shape[longest]
        spots.append(tuple(where))
    return result.at[spots[0]].set(smallest).at[spots[1]].set(largest)


def block_scale(key, extent, split, low, high):
    loudness, own = 1.0, jax.random.fold_in(key, 6)
    for position, parts in split:
        heights = jnp.exp(jax.random.uniform(jax.random.fold_in(own, position), (parts,), jnp.float32, low / len(split), high / len(split)))
        loudness = loudness * jnp.repeat(heights, extent[position] // parts).reshape([-1 if axis == position else 1 for axis in range(len(extent))])
    return loudness


def gaussian(own_key, dims, scale, limit, pieces=(), held_as=jnp.bfloat16):
    factor_of = block_scale(own_key, dims, pieces, -0.22, 0.18) if pieces else 1.0
    drawn = jax.random.normal(own_key, dims, jnp.float32) * scale * factor_of
    return jnp.minimum(jnp.maximum(drawn, -limit), limit).astype(held_as)


def setup_inputs(seed: int = 0) -> dict:
    keys = jax.random.split(jax.random.key(seed), 14)
    first_guess = gaussian(keys[0], (NSUB, NLON, C, LAT), 1.0, 6.0, ((0, 8), (1, 32)), jnp.float32)
    background = gaussian(keys[1], (NLON, C, LAT), 1.0, 6.0, ((0, 32),), jnp.float32)
    opening_kernel_matrix = gaussian(keys[2], (FEAT, 9 * C), (9 * C) ** -0.5, 0.21875)
    hidden_layer_shift = gaussian(keys[3], (FEAT,), 0.5, 3.0, (), jnp.float32)
    closing_kernel_matrix = gaussian(keys[4], (C, 9 * FEAT), (9 * FEAT) ** -0.5, 0.125)
    output_layer_shift = gaussian(keys[5], (C,), 0.3, 2.0, (), jnp.float32)
    model_weight = jnp.clip(jnp.exp(jax.random.uniform(keys[6], (C,), jnp.float32, math.log(0.5), math.log(2.0))), 0.5, 2.0)
    background_weight = jnp.clip(jnp.exp(jax.random.uniform(keys[7], (C,), jnp.float32, math.log(0.5), math.log(2.0))), 0.5, 2.0)
    obs_cell = set_ends(jax.random.randint(keys[8], (NSUB, OBS), 0, LON_DEV * LAT), jax.random.fold_in(keys[8], 1), 0, (LON_DEV * LAT) - 1).astype(jnp.int32)
    obs_chan = set_ends(jax.random.randint(keys[9], (NSUB, OBS), 0, C), jax.random.fold_in(keys[9], 1), 0, C - 1).astype(jnp.int32)
    obs_value = gaussian(keys[10], (NSUB, OBS), 1.0, 6.0, ((0, 8), (1, 32)), jnp.float32)
    obs_weight = jnp.clip(jnp.exp(math.log(4.0) - 2.0794415 * jax.random.uniform(keys[11], (NSUB, OBS), jnp.float32) ** block_scale(keys[11], (NSUB, OBS), ((0, 8), (1, 32)), -0.2, 0.2)), 0.5, 4.0)
    step_size = jnp.clip(jax.random.uniform(keys[12], (), jnp.float32, 0.3, 0.6), 0.3, 0.6)
    return dict(first_guess=first_guess, background=background, opening_kernel_matrix=opening_kernel_matrix, hidden_layer_shift=hidden_layer_shift, closing_kernel_matrix=closing_kernel_matrix, output_layer_shift=output_layer_shift, model_weight=model_weight, background_weight=background_weight, obs_cell=obs_cell, obs_chan=obs_chan, obs_value=obs_value, obs_weight=obs_weight, step_size=step_size)


def adjoint_weight(weight):
    rows_out = weight.shape[0]
    rows_in = weight.shape[1] // 9
    flipped = weight.reshape(rows_out, 3, 3, rows_in)[:, ::-1, ::-1, :]
    return flipped.transpose(3, 1, 2, 0).reshape(rows_in, 9 * rows_out)

def wrapped(field):
    return jnp.concatenate([field[-1:], field, field[:1]], axis=0)

def convolve(padded, weight):
    count = padded.shape[0] - 2
    lats = padded.shape[2]
    spread = jnp.pad(padded, ((0, 0), (0, 0), (1, 1)))
    stacked = jnp.concatenate([spread[a:a + count, :, b:b + lats] for a in range(3) for b in range(3)], axis=1)
    return jnp.einsum('fk,nkl->nfl', weight.astype(jnp.float32), stacked.astype(jnp.float32))

def propagate_onestep(system_vector, opening_kernel_matrix, hidden_layer_shift, closing_kernel_matrix, output_layer_shift):
    nonlinear_argument = convolve(wrapped(system_vector.astype(jnp.bfloat16)), opening_kernel_matrix) + hidden_layer_shift[None, :, None]
    hidden = jax.nn.gelu(nonlinear_argument).astype(jnp.bfloat16)
    return (system_vector + convolve(wrapped(hidden), closing_kernel_matrix) + output_layer_shift[None, :, None], nonlinear_argument)

def pullback(cotangent, nonlinear_argument, w_in_adj, w_out_adj):
    inner = convolve(wrapped(cotangent.astype(jnp.bfloat16)), w_out_adj)
    scaled = jax.vjp(jax.nn.gelu, nonlinear_argument)[1](inner)[0].astype(jnp.bfloat16)
    return cotangent + convolve(wrapped(scaled), w_in_adj)

def reference(first_guess, background, opening_kernel_matrix, hidden_layer_shift, closing_kernel_matrix, output_layer_shift, model_weight, background_weight, obs_cell, obs_chan, obs_value, obs_weight, step_size):
    subs, lons, chans, lats = first_guess.shape
    w_in_adj = adjoint_weight(opening_kernel_matrix)
    w_out_adj = adjoint_weight(closing_kernel_matrix)
    model_scale = model_weight[None, None, :, None]
    back_scale = background_weight[:, None]
    column = jnp.arange(obs_cell.shape[1], dtype=jnp.int32)[None, :]
    longitude = column // OBS_DEV * LON_DEV + obs_cell // lats
    flat = (longitude * (chans * lats) + obs_chan * lats + obs_cell % lats).astype(jnp.int32)
    rows = jnp.broadcast_to(jnp.arange(subs, dtype=jnp.int32)[:, None], flat.shape)
    valid = (jnp.arange(subs) > 0).astype(jnp.float32)[:, None, None, None]
    total = float(subs * lons * chans * lats)
    system_vector = first_guess
    costs = []
    for step in range(ITERS):
        propagate_trajectory, nonlinear_argument = lax.map(lambda present_iterate: propagate_onestep(present_iterate, opening_kernel_matrix, hidden_layer_shift, closing_kernel_matrix, output_layer_shift), system_vector)
        earlier_iterate = jnp.concatenate([jnp.zeros_like(propagate_trajectory[:1]), propagate_trajectory[:-1]], axis=0)
        defect = system_vector - earlier_iterate
        forcing = model_scale * defect * valid
        later = jnp.concatenate([forcing[1:], jnp.zeros_like(forcing[:1])], axis=0)
        pulled = lax.map(lambda t: pullback(t[0], t[1], w_in_adj, w_out_adj), (later, nonlinear_argument))
        estimate = jnp.take_along_axis(system_vector.reshape(subs, -1), flat, axis=1)
        misfit = estimate - obs_value
        weighted = obs_weight * misfit
        observed = jnp.zeros((subs, lons * chans * lats), jnp.float32).at[rows, flat].add(weighted).reshape(system_vector.shape)
        departure = system_vector[0] - background
        back_term = jnp.zeros_like(system_vector).at[0].set(back_scale * departure)
        gradient = forcing - pulled + observed + back_term
        cost = 0.5 * (jnp.sum(forcing * defect) + jnp.sum(weighted * misfit) + jnp.sum(back_scale * departure * departure))
        costs.append(cost)
        norm = jnp.sum(gradient * gradient)
        system_vector = system_vector - step_size / jnp.sqrt(norm / total + 1e-06) * gradient
    return (system_vector, jnp.stack(costs))
```

```python
import jax
import jax.numpy as jnp
from jax import lax
from jax.experimental import pallas as pl
from jax.experimental.pallas import tpu as pltpu
from jax.sharding import Mesh
from jax.sharding import PartitionSpec as P

LON = ("lon_0", "lon_1", "lon_2")
TM = ("tm_0", "tm_1")
TM_LON = TM + LON
C = 80
F = 256
LAT = 64
BAND = 8
HALO = 4
OBS = 256
W2 = 2 * LAT
F32 = jnp.float32
BF16 = jnp.bfloat16
KC = 0.7978845608028654


def lanes(rows=C):
    return lax.broadcasted_iota(jnp.int32, (rows, W2), 1)


def call(kernel, outs, scratch=(), specs=None):
    return pl.pallas_call(
        kernel,
        out_shape=outs,
        **({} if specs is None else {"in_specs": specs}),
        scratch_shapes=scratch,
        compiler_params=pltpu.CompilerParams(vmem_limit_bytes=48 << 20),
    )


def out(shape, dtype=F32):
    return jax.ShapeDtypeStruct(shape, dtype)


def dot(a, b):
    return jnp.dot(a, b, preferred_element_type=F32)


def earlier_lat(v):
    lane = lanes(v.shape[0])
    return jnp.where((lane == 0) | (lane == LAT), 0.0, pltpu.roll(v, 1, 1))


def later_lat(v):
    lane = lanes(v.shape[0])
    return jnp.where((lane == LAT - 1) | (lane == W2 - 1), 0.0, pltpu.roll(v, W2 - 1, 1))


def halves(v):
    return pltpu.roll(v, LAT, 1)


def pack_kernel(x_ref, bg_ref, xp_ref, xl_ref, xr_ref, bgp_ref):
    for i in range(BAND):
        v = jnp.concatenate([x_ref[0, i], x_ref[1, i]], axis=1)
        xp_ref[i] = v
        half = xl_ref if i < HALO else xr_ref
        half[i % HALO] = v.astype(BF16)
        bgp_ref[i] = jnp.concatenate([bg_ref[i], jnp.zeros((C, LAT), F32)], axis=1)


def pack(x, bg):
    edge = out((HALO, C, W2), BF16)
    full = out((BAND, C, W2))
    return call(pack_kernel, (full, edge, edge, full))(x, bg)


def weights_kernel(o_ref, c_ref, b1_ref, b2_ref, mw_ref, bw_ref,
                   k2_ref, wia_ref, woa_ref, bias_ref, small_ref, wide, tall, row):
    wide[:, 9 * C :] = jnp.zeros((F, 768 - 9 * C), F32)
    wide[:, : 9 * C] = o_ref[...].astype(F32)
    turned = wide[...].T
    tall[9 * C :, :] = jnp.zeros((768 - 9 * C, F), F32)
    for t in range(9):
        a, b = divmod(t, 3)
        block = c_ref[:, F * t : F * (t + 1)]
        k2_ref[C * b : C * (b + 1), F * a : F * (a + 1)] = block
        tall[C * (8 - t) : C * (9 - t), :] = block.astype(F32)
        wia_ref[C * b : C * (b + 1), F * a : F * (a + 1)] = turned[C * (8 - t) : C * (9 - t)].astype(BF16)
    back = tall[...].T
    woa_ref[...] = back[:, : 9 * C].astype(BF16)
    bias_ref[...] = jnp.broadcast_to(b1_ref[...], (W2, F)).T
    row[...] = jnp.zeros((W2, W2), F32)
    for n, ref in enumerate((b2_ref, mw_ref, bw_ref)):
        row[:, :C] = jnp.broadcast_to(ref[...], (W2, C))
        small_ref[n] = row[...].T[:C]


def prepare_weights(opening, closing, b1, b2, mw, bw):
    return call(
        weights_kernel,
        (out((3 * C, 3 * F), BF16), out((3 * C, 3 * F), BF16), out((F, 9 * C), BF16), out((F, W2)), out((3, C, W2))),
        [pltpu.VMEM((F, 768), F32), pltpu.VMEM((768, F), F32), pltpu.VMEM((W2, W2), F32)],
    )(opening, closing, b1[None], b2[None], mw[None], bw[None])


def split3(v):
    hi = v.astype(BF16)
    rest = v - hi.astype(F32)
    mid = rest.astype(BF16)
    low = (rest - mid.astype(F32)).astype(BF16)
    return jnp.concatenate([hi, mid, low], axis=0)


def join3(v):
    return (v[2 * C :] + v[C : 2 * C]) + v[:C]


def obs_kernel(cell_ref, chan_ref, val_ref, wt_ref, x_ref, r_ref, s_ref, hot):
    def line(ref):
        return jnp.concatenate([ref[0:1, :], ref[1:2, :]], axis=1)

    cell = line(cell_ref)
    sub = (lax.broadcasted_iota(jnp.int32, cell.shape, 1) >= OBS).astype(jnp.int32)
    spot = (cell >> 6) * W2 + sub * LAT + (cell & (LAT - 1))
    rows = 2 * W2
    for p in range(BAND // 2):
        at = lax.broadcasted_iota(jnp.int32, (rows, 2 * OBS), 0) + p * rows
        hot[p] = jnp.where(at == spot, 1.0, 0.0).astype(BF16)
    total = jnp.zeros((3 * C, 2 * OBS), F32)
    for p in range(BAND // 2):
        total = total + dot(split3(jnp.concatenate([x_ref[2 * p], x_ref[2 * p + 1]], axis=1)), hot[p])
    mine = lax.broadcasted_iota(jnp.int32, (C, 2 * OBS), 0) == line(chan_ref)
    r = jnp.sum(jnp.where(mine, join3(total), 0.0), axis=0, keepdims=True) - line(val_ref)
    r_ref[0:1, :] = r[:, :OBS]
    r_ref[1:2, :] = r[:, OBS:]
    spread = split3(jnp.where(mine, line(wt_ref) * r, 0.0))
    for p in range(BAND // 2):
        got = lax.dot_general(spread, hot[p], (((1,), (1,)), ((), ())), preferred_element_type=F32)
        got = join3(got)
        s_ref[2 * p] = got[:, :W2]
        s_ref[2 * p + 1] = got[:, W2:]


def observe(cell, chan, val, wt, field):
    return call(
        obs_kernel,
        (out((2, OBS)), out((BAND, C, W2))),
        [pltpu.VMEM((BAND // 2, 2 * W2, 2 * OBS), BF16)],
    )(cell, chan, val, wt, field)


def strip_kernel(l_ref, a_ref, b_ref, r_ref, up_ref, down_ref):
    def at(e):
        if e < 0:
            return l_ref[HALO + e].astype(F32)
        if e < HALO:
            return a_ref[e].astype(F32)
        if e < BAND:
            return b_ref[e - HALO].astype(F32)
        return r_ref[e - BAND].astype(F32)

    left = lanes() < LAT
    for p in range(6):
        one, two = at(p - 2), at(p + 4)
        up_ref[p] = jnp.where(left, one, halves(two)).astype(BF16)
        down_ref[p] = jnp.where(left, halves(one), two).astype(BF16)


def strips(from_left, mine_left, mine_right, from_right):
    strip = out((6, C, W2), BF16)
    return call(strip_kernel, (strip, strip))(from_left, mine_left, mine_right, from_right)


def gelu_pair(v):
    sq = v * v
    t = jnp.tanh(v * (KC + (KC * 0.044715) * sq))
    half = 0.5 * (1.0 + t)
    slope = half + (0.5 * v) * (1.0 - t * t) * (KC + (3 * KC * 0.044715) * sq)
    return v * half, slope


def stack_lats(ref, n, v):
    ref[3 * C * n : 3 * C * n + C] = earlier_lat(v).astype(BF16)
    ref[3 * C * n + C : 3 * C * n + 2 * C] = v.astype(BF16)
    ref[3 * C * n + 2 * C : 3 * C * n + 3 * C] = later_lat(v).astype(BF16)


def window(ref, n, rows):
    return jnp.concatenate([ref[rows * n : rows * (n + 3)], ref[rows * (n + 1) : rows * (n + 4)]], axis=1)


def sum_lats(s):
    res = []
    for k in range(2):
        part = s[:, W2 * k : W2 * (k + 1)]
        res.append(earlier_lat(part[:C]) + part[C : 2 * C] + later_lat(part[2 * C :]))
    return res


def step_from(sums, step, total):
    whole = jnp.sum(sums, axis=0, keepdims=True)
    lane = lax.broadcasted_iota(jnp.int32, whole.shape, 1)
    norm = jnp.sum(jnp.where(lane == 0, whole, 0.0), axis=1, keepdims=True)
    return step / jnp.sqrt(norm / total + 1e-06)


def gradient_kernel(total, second, n_tm, n_all):
    def kernel(*refs):
        refs = list(refs)
        place_ref = refs.pop(0)
        base = [refs.pop(0) for _ in range(7)]
        if second:
            step_ref, sums_ref = refs.pop(0), refs.pop(0)
            grad = [refs.pop(0) for _ in range(7)]
        bg_ref, wt_ref, o_ref, k2_ref, wia_ref, woa_ref, bias_ref, small_ref = [refs.pop(0) for _ in range(8)]
        g_ref, gl_ref, gr_ref, row_ref = [refs.pop(0) for _ in range(4)]
        x1_ref = refs.pop(0) if second else None
        vx, hid, slope, vl, x_ext, ln = refs
        place = place_ref[0]
        alpha = step_from(sums_ref[...], step_ref[0], total) if second else None

        def state(which, n):
            v = base[which][n].astype(F32)
            if second:
                v = v - alpha * grad[which][n].astype(F32)
            return v

        own, lft, rgt, upp, dwn, obs, res = range(7)
        left = lanes() < LAT
        for e in range(16):
            v = state(lft, e) if e < HALO else state(own, e - HALO) if e < HALO + BAND else state(rgt, e - HALO - BAND)
            x_ext[e] = v
            if second and HALO <= e < HALO + BAND:
                x1_ref[e - HALO] = v
            stack_lats(vx, e, v)
        bias = bias_ref[...]
        bias2 = jnp.concatenate([bias, bias], axis=1)
        b2 = small_ref[0]
        mw = small_ref[1]
        bw = small_ref[2]
        for h in range(0, 14, 2):
            pre = dot(o_ref[...], window(vx, h, 3 * C)) + bias2
            act, sl = gelu_pair(pre)
            for k in range(2):
                n = h + k
                hid[F * n : F * (n + 1)] = act[:, W2 * k : W2 * (k + 1)].astype(BF16)
                if 2 <= n < 12:
                    slope[n - 2] = sl[:, W2 * k : W2 * (k + 1)]
        for o in range(0, 12, 2):
            s = sum_lats(dot(k2_ref[...], window(hid, o, F)))
            for k in range(2):
                n = o + k
                x = x_ext[n + 2]
                m = x + s[k] + b2
                u = state(upp, n % 6)
                nxt = jnp.where(left, halves(x), u if n >= 6 else halves(u))
                keep = left | (place < n_tm - 1)
                lv = jnp.where(keep, mw * (nxt - m), 0.0)
                ln[n] = lv
                stack_lats(vl, n, lv)
        for h in range(0, 10, 2):
            z = dot(woa_ref[...], window(vl, h, 3 * C))
            for k in range(2):
                n = h + k
                hid[F * n : F * (n + 1)] = (slope[n] * z[:, W2 * k : W2 * (k + 1)]).astype(BF16)
        for o in range(0, BAND, 2):
            s = sum_lats(dot(wia_ref[...], window(hid, o, F)))
            for k in range(2):
                g_ref[o + k] = ln[o + k + 2] + s[k]
        for r in range(8):
            one = state(dwn, r) if r < 6 else halves(state(dwn, r - 6))
            two = state(dwn, r - 2) if r >= 2 else halves(state(dwn, r + 4))
            v = jnp.where(left, one, two)
            x_ext[r] = v
            stack_lats(vx, r, v)
        for h in range(0, 6, 2):
            act, _ = gelu_pair(dot(o_ref[...], window(vx, h, 3 * C)) + bias2)
            for k in range(2):
                n = h + k
                hid[F * n : F * (n + 1)] = act[:, W2 * k : W2 * (k + 1)].astype(BF16)
        squares = jnp.zeros((C, W2), F32)
        cost = jnp.zeros((C, W2), F32)
        for o in range(0, 4, 2):
            s = sum_lats(dot(k2_ref[...], window(hid, o, F)))
            for k in range(2):
                m = x_ext[o + k + 2] + s[k] + b2
                for side in range(2):
                    i = o + k + 4 * side
                    x = state(own, i)
                    before = m if side == 0 else halves(m)
                    first = jnp.where(place > 0, mw * (x - before), 0.0)
                    lo = jnp.where(left, first, halves(ln[i + 2]))
                    dep = jnp.where(left & (place == 0), x - bg_ref[i], 0.0)
                    g = lo - g_ref[i] + state(obs, i) + bw * dep
                    g_ref[i] = g
                    edge = gl_ref if i < HALO else gr_ref
                    edge[i % HALO] = g.astype(BF16)
                    squares = squares + g * g
                    cost = cost + lo * lo / mw + bw * dep * dep
        r = base[res][...]
        if second:
            r = r - alpha * grad[res][...]
        paid = jnp.sum(jnp.sum(wt_ref[...] * r * r, axis=0, keepdims=True), axis=1, keepdims=True)
        norm = jnp.sum(jnp.sum(squares, axis=0, keepdims=True), axis=1, keepdims=True)
        paid = 0.5 * (paid + jnp.sum(jnp.sum(cost, axis=0, keepdims=True), axis=1, keepdims=True))
        lane = lax.broadcasted_iota(jnp.int32, (n_all, W2), 1)
        row_ref[...] = jnp.where(lane == 0, norm, jnp.where(lane == 1, paid, 0.0))

    return kernel


def gradient(total, n_tm, n_all, place, base, extra, consts):
    second = extra is not None
    smem = pl.BlockSpec(memory_space=pltpu.SMEM)
    vmem = pl.BlockSpec(memory_space=pltpu.VMEM)
    args = [place] + list(base)
    specs = [smem] + [vmem] * 7
    if second:
        step, sums, grads = extra
        args += [step, sums] + list(grads)
        specs += [smem] + [vmem] * 8
    args += list(consts)
    specs += [vmem] * len(consts)
    full = out((BAND, C, W2))
    edge = out((HALO, C, W2), BF16)
    outs = [full, edge, edge, out((n_all, W2))] + ([full] if second else [])
    return call(
        gradient_kernel(total, second, n_tm, n_all),
        tuple(outs),
        [
            pltpu.VMEM((16 * 3 * C, W2), BF16),
            pltpu.VMEM((14 * F, W2), BF16),
            pltpu.VMEM((10, F, W2), F32),
            pltpu.VMEM((12 * 3 * C, W2), BF16),
            pltpu.VMEM((16, C, W2), F32),
            pltpu.VMEM((12, C, W2), F32),
        ],
        specs,
    )(*args)


def final_kernel(total):
    def kernel(step_ref, first_ref, sums_ref, x_ref, g_ref, x_out, cost_out):
        alpha = step_from(sums_ref[...], step_ref[0], total)
        for i in range(BAND):
            v = x_ref[i] - alpha * g_ref[i]
            x_out[0, i] = v[:, :LAT]
            x_out[1, i] = v[:, LAT:]
        c0 = jnp.sum(first_ref[...], axis=0, keepdims=True)
        c1 = jnp.sum(sums_ref[...], axis=0, keepdims=True)
        lane = lax.broadcasted_iota(jnp.int32, c0.shape, 1)
        one = jnp.sum(jnp.where(lane == 1, c0, 0.0), axis=1, keepdims=True)
        two = jnp.sum(jnp.where(lane == 1, c1, 0.0), axis=1, keepdims=True)
        cost_out[...] = jnp.where(lane == 0, one, two)[:, :2]

    return kernel


def shifted(value, axes, by, closed):
    n = lax.axis_size(axes)
    pairs = [(i, (i + by) % n) for i in range(n) if closed or 0 <= i + by < n]
    return lax.ppermute(value, axes, pairs)


def exchange(mine_left, mine_right):
    from_right = shifted(mine_left, LON, -1, True)
    from_left = shifted(mine_right, LON, 1, True)
    up, down = strips(from_left, mine_left, mine_right, from_right)
    after = shifted(up, TM, -1, False)
    before = shifted(down, TM, 1, False)
    return from_left, from_right, after, before


def per_device(x, background, opening, b1, closing, b2, mw, bw, cell, chan, val, wt, step):
    n_tm = lax.axis_size(TM)
    n_all = n_tm * lax.axis_size(LON)
    total = float(2 * BAND * C * LAT * n_all)
    place = lax.axis_index(TM).astype(jnp.int32)[None]
    step = step[None]
    xp, xl, xr, bgp = pack(x, background)
    halo = exchange(xl, xr)
    k2, wia, woa, bias, small = prepare_weights(opening, closing, b1, b2, mw, bw)
    r0, s0 = observe(cell, chan, val, wt, xp)
    consts = (bgp, wt, opening, k2, wia, woa, bias, small)
    base = (xp,) + halo + (s0, r0)
    g0, gl, gr, row = gradient(total, n_tm, n_all, place, base, None, consts)
    ghalo = exchange(gl, gr)
    sums0 = lax.all_to_all(row, TM_LON, 0, 0, tiled=True)
    rg, sg = observe(cell, chan, jnp.zeros_like(val), wt, g0)
    grads = (g0,) + ghalo + (sg, rg)
    g1, _, _, row, x1 = gradient(total, n_tm, n_all, place, base, (step, sums0, grads), consts)
    sums1 = lax.all_to_all(row, TM_LON, 0, 0, tiled=True)
    smem = pl.BlockSpec(memory_space=pltpu.SMEM)
    vmem = pl.BlockSpec(memory_space=pltpu.VMEM)
    x2, costs = call(
        final_kernel(total), (out((2, BAND, C, LAT)), out((1, 2))), specs=[smem] + [vmem] * 4
    )(step, sums0, sums1, x1, g1)
    return x2, costs.reshape(2)


def solution(mesh):
    n_tm, n_lon = mesh.devices.shape
    if (n_tm, n_lon) == (8, 32):
        shape = (4, 2, 2, 8, 2)
    else:
        shape = (n_tm, 1, 1, n_lon // 2, 2)
    split = Mesh(mesh.devices.reshape(shape), TM_LON)
    placed = (
        P(TM, LON, None, None),
        P(LON, None, None),
        P(), P(), P(), P(), P(), P(),
        P(TM, LON), P(TM, LON), P(TM, LON), P(TM, LON),
        P(),
    )
    return jax.shard_map(
        per_device,
        mesh=split,
        in_specs=placed,
        out_specs=(P(TM, LON, None, None), P()),
        check_vma=False,
    )
```

```python
import functools

import jax
import jax.numpy as jnp
from jax import lax
from jax.experimental import pallas as pl
from jax.experimental.pallas import tpu as pltpu
from jax.sharding import Mesh
from jax.sharding import PartitionSpec as P


LON = ("lon_0", "lon_1", "lon_2")
TM = ("tm_0", "tm_1")
TM_LON = TM + LON
C = 80
F = 256
LAT = 64
BAND = 8
HALO = 4
OBS = 256
W2 = 2 * LAT
F32 = jnp.float32
BF16 = jnp.bfloat16
KC = 0.7978845608028654


def lanes(rows=C):
    return lax.broadcasted_iota(jnp.int32, (rows, W2), 1)


def call(kernel, ins, outs, scratch=(), limit=8, scalars=0):
    smem = pl.BlockSpec(memory_space=pltpu.SMEM)
    vmem = pl.BlockSpec(memory_space=pltpu.VMEM)
    return pl.pallas_call(
        kernel,
        out_shape=tuple(jax.ShapeDtypeStruct(shape, dtype) for shape, dtype in outs),
        in_specs=[smem] * scalars + [vmem] * (len(ins) - scalars),
        out_specs=tuple(vmem for _ in outs),
        scratch_shapes=list(scratch),
        compiler_params=pltpu.CompilerParams(vmem_limit_bytes=limit << 20),
    )(*ins)


def dot(a, b):
    return jnp.dot(a, b, preferred_element_type=F32)


def earlier_lat(v):
    lane = lanes(v.shape[0])
    return jnp.where((lane == 0) | (lane == LAT), 0.0, pltpu.roll(v, 1, 1))


def later_lat(v):
    lane = lanes(v.shape[0])
    return jnp.where((lane == LAT - 1) | (lane == W2 - 1), 0.0, pltpu.roll(v, W2 - 1, 1))


def halves(v):
    return pltpu.roll(v, LAT, 1)


def pack_kernel(place_ref, step_ref, x_ref, xp_ref, xl_ref, xr_ref, place_row, step_row):
    place_row[...] = jnp.full((1, W2), place_ref[0], jnp.int32)
    step_row[...] = jnp.full((1, W2), step_ref[0], F32)
    for i in range(BAND):
        v = jnp.concatenate([x_ref[0, i], x_ref[1, i]], axis=0).T
        xp_ref[i] = v
        half = xl_ref if i < HALO else xr_ref
        half[i % HALO] = v.astype(BF16)


def pack(place, step, x):
    edge = ((HALO, C, W2), BF16)
    outs = [((BAND, C, W2), F32), edge, edge, ((1, W2), jnp.int32), ((1, W2), F32)]
    return call(pack_kernel, [place, step, x], outs, scalars=2)


def weights_kernel(ot_ref, c_ref, b1_ref, b2_ref, mw_ref, bw_ref, bg_ref,
                   o_ref, k2_ref, wia_ref, woa_ref, bias_ref, small_ref, bgp_ref, tall, row):
    tall[9 * C :, :] = jnp.zeros((768 - 9 * C, F), F32)
    tall[: 9 * C, :] = ot_ref[...].astype(F32)
    o_ref[...] = tall[...].T[:, : 9 * C].astype(BF16)
    turned = ot_ref
    for t in range(9):
        a, b = divmod(t, 3)
        block = c_ref[:, F * t : F * (t + 1)]
        k2_ref[C * b : C * (b + 1), F * a : F * (a + 1)] = block
        tall[C * (8 - t) : C * (9 - t), :] = block.astype(F32)
        wia_ref[C * b : C * (b + 1), F * a : F * (a + 1)] = turned[C * (8 - t) : C * (9 - t), :]
    back = tall[...].T
    woa_ref[...] = back[:, : 9 * C].astype(BF16)
    bias_ref[...] = jnp.broadcast_to(b1_ref[...], (W2, F)).T
    row[...] = jnp.zeros((W2, W2), F32)
    for n, ref in enumerate((b2_ref, mw_ref, bw_ref)):
        row[:, :C] = jnp.broadcast_to(ref[...], (W2, C))
        small_ref[n] = row[...].T[:C]
    for i in range(BAND):
        bgp_ref[i] = jnp.concatenate([bg_ref[i], jnp.zeros((LAT, C), F32)], axis=0).T


def prepare_weights(opening_t, closing, b1, b2, mw, bw, bg):
    ins = [opening_t, closing, b1[None], b2[None], mw[None], bw[None], bg]
    outs = [((F, 9 * C), BF16), ((3 * C, 3 * F), BF16), ((3 * C, 3 * F), BF16), ((F, 9 * C), BF16)]
    outs += [((F, W2), F32), ((3, C, W2), F32), ((BAND, C, W2), F32)]
    return call(
        weights_kernel,
        ins,
        outs,
        [pltpu.VMEM((768, F), F32), pltpu.VMEM((W2, W2), F32)],
    )


def split3(v):
    hi = v.astype(BF16)
    rest = v - hi.astype(F32)
    mid = rest.astype(BF16)
    low = (rest - mid.astype(F32)).astype(BF16)
    return jnp.concatenate([hi, mid, low], axis=0)


def join3(v):
    return (v[2 * C :] + v[C : 2 * C]) + v[:C]


def obs_kernel(cell_ref, chan_ref, val_ref, wt_ref, x_ref, r_ref, s_ref, hot, plain=False):
    def line(ref):
        return jnp.concatenate([ref[0:1, :], ref[1:2, :]], axis=1)

    cell = line(cell_ref)
    sub = (lax.broadcasted_iota(jnp.int32, cell.shape, 1) >= OBS).astype(jnp.int32)
    spot = (cell >> 6) * W2 + sub * LAT + (cell & (LAT - 1))
    rows = 2 * W2
    for p in range(BAND // 2):
        at = lax.broadcasted_iota(jnp.int32, (rows, 2 * OBS), 0) + p * rows
        hot[p] = jnp.where(at == spot, 1.0, 0.0).astype(BF16)
    total = jnp.zeros((3 * C, 2 * OBS), F32)
    for p in range(BAND // 2):
        total = total + dot(split3(jnp.concatenate([x_ref[2 * p], x_ref[2 * p + 1]], axis=1)), hot[p])
    mine = lax.broadcasted_iota(jnp.int32, (C, 2 * OBS), 0) == line(chan_ref)
    r = jnp.sum(jnp.where(mine, join3(total), 0.0), axis=0, keepdims=True)
    if not plain:
        r = r - line(val_ref)
    r_ref[0:1, :] = r[:, :OBS]
    r_ref[1:2, :] = r[:, OBS:]
    spread = split3(jnp.where(mine, line(wt_ref) * r, 0.0))
    for p in range(BAND // 2):
        got = lax.dot_general(spread, hot[p], (((1,), (1,)), ((), ())), preferred_element_type=F32)
        got = join3(got)
        s_ref[2 * p] = got[:, :W2]
        s_ref[2 * p + 1] = got[:, W2:]


def observe(cell, chan, val, wt, field, plain):
    return call(
        functools.partial(obs_kernel, plain=plain),
        [cell, chan, val, wt, field],
        [((2, OBS), F32), ((BAND, C, W2), F32)],
        [pltpu.VMEM((BAND // 2, 2 * W2, 2 * OBS), BF16)],
    )


def strip_kernel(l_ref, a_ref, b_ref, r_ref, up_ref, down_ref):
    def at(e):
        if e < 0:
            return l_ref[HALO + e].astype(F32)
        if e < HALO:
            return a_ref[e].astype(F32)
        if e < BAND:
            return b_ref[e - HALO].astype(F32)
        return r_ref[e - BAND].astype(F32)

    left = lanes() < LAT
    for p in range(6):
        one, two = at(p - 2), at(p + 4)
        up_ref[p] = jnp.where(left, one, halves(two)).astype(BF16)
        down_ref[p] = jnp.where(left, halves(one), two).astype(BF16)


def strips(from_left, mine_left, mine_right, from_right):
    strip = ((6, C, W2), BF16)
    return call(strip_kernel, [from_left, mine_left, mine_right, from_right], [strip, strip])


def gelu_pair(v):
    sq = v * v
    t = jnp.tanh(v * (KC + (KC * 0.044715) * sq))
    half = 0.5 * (1.0 + t)
    slope = half + (0.5 * v) * (1.0 - t * t) * (KC + (3 * KC * 0.044715) * sq)
    return v * half, slope


def stack_lats(ref, n, v):
    ref[3 * C * n : 3 * C * n + C] = earlier_lat(v).astype(BF16)
    ref[3 * C * n + C : 3 * C * n + 2 * C] = v.astype(BF16)
    ref[3 * C * n + 2 * C : 3 * C * n + 3 * C] = later_lat(v).astype(BF16)


def window(ref, n, rows):
    return jnp.concatenate([ref[rows * n : rows * (n + 3)], ref[rows * (n + 1) : rows * (n + 4)]], axis=1)


def sum_lats(s):
    res = []
    for k in range(2):
        part = s[:, W2 * k : W2 * (k + 1)]
        res.append(earlier_lat(part[:C]) + part[C : 2 * C] + later_lat(part[2 * C :]))
    return res


def step_from(sums, step, total):
    whole = jnp.sum(sums, axis=0, keepdims=True)
    lane = lax.broadcasted_iota(jnp.int32, whole.shape, 1)
    norm = jnp.sum(jnp.where(lane == 0, whole, 0.0), axis=1, keepdims=True)
    return step[:, :1] / jnp.sqrt(norm / total + 1e-06)


def gradient_kernel(total, second, n_tm, n_all):
    def kernel(*refs):
        refs = list(refs)
        take = lambda n: [refs.pop(0) for _ in range(n)]
        (place_ref,) = take(1)
        if second:
            step_ref, sums_ref = take(2)
            g0_ref, glft, grgt, upp1, dwn1, r1_ref, s1_ref = take(7)
        own_ref, lft, rgt, upp0, dwn0, r0_ref, s0_ref = take(7)
        bg_ref, wt_ref, o_ref, k2_ref, wia_ref, woa_ref, bias_ref, small_ref = take(8)
        if second:
            g_ref, x1_ref, row_ref = take(3)
        else:
            g_ref, gl_ref, gr_ref, row_ref = take(4)
        vx, hid, slope, vl, x_ext, x_prev, ln, gh = refs
        place = place_ref[...]
        left = lanes() < LAT
        if second:
            alpha = step_from(sums_ref[...], step_ref[...], total)

            def upp(n):
                return upp0[n].astype(F32) - alpha * upp1[n].astype(F32)

            def dwn(n):
                return dwn0[n].astype(F32) - alpha * dwn1[n].astype(F32)

            def obs(n):
                return s0_ref[n] - alpha * s1_ref[n]

            for e in range(16):
                v = lft[e] if e < HALO else own_ref[e - HALO] if e < HALO + BAND else rgt[e - HALO - BAND]
                g = glft[e] if e < HALO else g0_ref[e - HALO] if e < HALO + BAND else grgt[e - HALO - BAND]
                v = v.astype(F32) - alpha * g.astype(F32)
                x_ext[e] = v
                if HALO <= e < HALO + BAND:
                    x1_ref[e - HALO] = v
                stack_lats(vx, e, v)
        else:

            def upp(n):
                return upp0[n].astype(F32)

            def dwn(n):
                return dwn0[n].astype(F32)

            def obs(n):
                return s0_ref[n]

            for e in range(16):
                v = lft[e] if e < HALO else own_ref[e - HALO] if e < HALO + BAND else rgt[e - HALO - BAND]
                v = v.astype(F32)
                x_ext[e] = v
                stack_lats(vx, e, v)
        bias = bias_ref[...]
        bias2 = jnp.concatenate([bias, bias], axis=1)
        b2 = small_ref[0]
        mw = small_ref[1]
        bw = small_ref[2]
        for h in range(0, 14, 2):
            pre = dot(o_ref[...], window(vx, h, 3 * C)) + bias2
            act, sl = gelu_pair(pre)
            for k in range(2):
                n = h + k
                hid[F * n : F * (n + 1)] = act[:, W2 * k : W2 * (k + 1)].astype(BF16)
                if 2 <= n < 12:
                    slope[n - 2] = sl[:, W2 * k : W2 * (k + 1)]
        for o in range(0, 12, 2):
            s = sum_lats(dot(k2_ref[...], window(hid, o, F)))
            for k in range(2):
                n = o + k
                x = x_ext[n + 2]
                m = x + s[k] + b2
                u = upp(n % 6)
                nxt = jnp.where(left, halves(x), u if n >= 6 else halves(u))
                keep = left | (place < n_tm - 1)
                lv = jnp.where(keep, mw * (nxt - m), 0.0)
                ln[n] = lv
                stack_lats(vl, n, lv)
        for h in range(0, 10, 2):
            z = dot(woa_ref[...], window(vl, h, 3 * C))
            for k in range(2):
                n = h + k
                hid[F * n : F * (n + 1)] = (slope[n] * z[:, W2 * k : W2 * (k + 1)]).astype(BF16)
        for o in range(0, BAND, 2):
            s = sum_lats(dot(wia_ref[...], window(hid, o, F)))
            for k in range(2):
                gh[o + k] = ln[o + k + 2] + s[k]
        for r in range(8):
            one = dwn(r) if r < 6 else halves(dwn(r - 6))
            two = dwn(r - 2) if r >= 2 else halves(dwn(r + 4))
            v = jnp.where(left, one, two)
            x_prev[r] = v
            stack_lats(vx, r, v)
        for h in range(0, 6, 2):
            act, _ = gelu_pair(dot(o_ref[...], window(vx, h, 3 * C)) + bias2)
            for k in range(2):
                n = h + k
                hid[F * n : F * (n + 1)] = act[:, W2 * k : W2 * (k + 1)].astype(BF16)
        squares = jnp.zeros((C, W2), F32)
        cost = jnp.zeros((C, W2), F32)
        for o in range(0, 4, 2):
            s = sum_lats(dot(k2_ref[...], window(hid, o, F)))
            for k in range(2):
                m = x_prev[o + k + 2] + s[k] + b2
                for side in range(2):
                    i = o + k + 4 * side
                    x = x_ext[i + HALO]
                    before = m if side == 0 else halves(m)
                    first = jnp.where(place > 0, mw * (x - before), 0.0)
                    lo = jnp.where(left, first, halves(ln[i + 2]))
                    dep = jnp.where(left & (place == 0), x - bg_ref[i], 0.0)
                    g = lo - gh[i] + obs(i) + bw * dep
                    g_ref[i] = g
                    if not second:
                        edge = gl_ref if i < HALO else gr_ref
                        edge[i % HALO] = g.astype(BF16)
                    squares = squares + g * g
                    cost = cost + lo * lo / mw + bw * dep * dep
        r = r0_ref[...]
        if second:
            r = r - alpha * r1_ref[...]
        paid = jnp.sum(jnp.sum(wt_ref[...] * r * r, axis=0, keepdims=True), axis=1, keepdims=True)
        norm = jnp.sum(jnp.sum(squares, axis=0, keepdims=True), axis=1, keepdims=True)
        paid = 0.5 * (paid + jnp.sum(jnp.sum(cost, axis=0, keepdims=True), axis=1, keepdims=True))
        lane = lax.broadcasted_iota(jnp.int32, (n_all, W2), 1)
        row_ref[...] = jnp.where(lane == 0, norm, jnp.where(lane == 1, paid, 0.0))

    return kernel


def gradient(total, n_tm, n_all, ins, second):
    full = ((BAND, C, W2), F32)
    edge = ((HALO, C, W2), BF16)
    row = ((n_all, W2), F32)
    outs = [full, full, row] if second else [full, edge, edge, row]
    return call(
        gradient_kernel(total, second, n_tm, n_all),
        ins,
        outs,
        [
            pltpu.VMEM((16 * 3 * C, W2), BF16),
            pltpu.VMEM((14 * F, W2), BF16),
            pltpu.VMEM((10, F, W2), F32),
            pltpu.VMEM((12 * 3 * C, W2), BF16),
            pltpu.VMEM((16, C, W2), F32),
            pltpu.VMEM((8, C, W2), F32),
            pltpu.VMEM((12, C, W2), F32),
            pltpu.VMEM((BAND, C, W2), F32),
        ],
        limit=24,
    )


def final_kernel(total):
    def kernel(step_ref, first_ref, sums_ref, x_ref, g_ref, x_out, cost_out):
        alpha = step_from(sums_ref[...], step_ref[...], total)
        for i in range(BAND):
            v = x_ref[i] - alpha * g_ref[i]
            v = jnp.concatenate([v, jnp.zeros((W2 - C, W2), F32)], axis=0).T[:, :C]
            x_out[0, i] = v[:LAT]
            x_out[1, i] = v[LAT:]
        c0 = jnp.sum(first_ref[...], axis=0, keepdims=True)
        c1 = jnp.sum(sums_ref[...], axis=0, keepdims=True)
        lane = lax.broadcasted_iota(jnp.int32, c0.shape, 1)
        one = jnp.sum(jnp.where(lane == 1, c0, 0.0), axis=1, keepdims=True)
        two = jnp.sum(jnp.where(lane == 1, c1, 0.0), axis=1, keepdims=True)
        cost_out[...] = jnp.where(lane == 0, one, two)[:, :2]

    return kernel


def shifted(value, axes, by, closed):
    n = lax.axis_size(axes)
    pairs = [(i, (i + by) % n) for i in range(n) if closed or 0 <= i + by < n]
    return lax.ppermute(value, axes, pairs)


def exchange(mine_left, mine_right):
    from_right = shifted(mine_left, LON, -1, True)
    from_left = shifted(mine_right, LON, 1, True)
    up, down = strips(from_left, mine_left, mine_right, from_right)
    after = shifted(up, TM, -1, False)
    before = shifted(down, TM, 1, False)
    return from_left, from_right, after, before


def per_device(x, background, opening, b1, closing, b2, mw, bw, cell, chan, val, wt, step):
    n_tm = lax.axis_size(TM)
    n_all = n_tm * lax.axis_size(LON)
    total = float(2 * BAND * C * LAT * n_all)
    place = lax.axis_index(TM).astype(jnp.int32)[None]
    step = step[None]
    xp, xl, xr, place, step = pack(place, step, jnp.swapaxes(x, 2, 3))
    halo = exchange(xl, xr)
    o, k2, wia, woa, bias, small, bgp = prepare_weights(
        opening.T, closing, b1, b2, mw, bw, jnp.swapaxes(background, 1, 2)
    )
    r0, s0 = observe(cell, chan, val, wt, xp, False)
    consts = (bgp, wt, o, k2, wia, woa, bias, small)
    base = (xp,) + halo + (r0, s0)
    g0, gl, gr, row = gradient(total, n_tm, n_all, (place,) + base + consts, False)
    ghalo = exchange(gl, gr)
    rg, sg = observe(cell, chan, val, wt, g0, True)
    row, rg, _, _ = lax.optimization_barrier((row, rg) + ghalo[:2])
    sums0 = lax.all_to_all(row, TM_LON, 0, 0, tiled=True)
    ins = (place, step, sums0, g0) + ghalo + (rg, sg) + base + consts
    g1, x1, row = gradient(total, n_tm, n_all, ins, True)
    sums1 = lax.all_to_all(row, TM_LON, 0, 0, tiled=True)
    x2, costs = call(
        final_kernel(total),
        [step, sums0, sums1, x1, g1],
        [((2, BAND, LAT, C), F32), ((1, 2), F32)],
    )
    return jnp.swapaxes(x2, 2, 3), costs.reshape(2)


def solution(mesh):
    n_tm, n_lon = mesh.devices.shape
    if (n_tm, n_lon) == (8, 32):
        shape = (4, 2, 2, 8, 2)
    else:
        shape = (n_tm, 1, 1, n_lon // 2, 2)
    split = Mesh(mesh.devices.reshape(shape), TM_LON)
    placed = (
        P(TM, LON, None, None),
        P(LON, None, None),
        P(), P(), P(), P(), P(), P(),
        P(TM, LON), P(TM, LON), P(TM, LON), P(TM, LON),
        P(),
    )
    return jax.shard_map(
        per_device,
        mesh=split,
        in_specs=placed,
        out_specs=(P(TM, LON, None, None), P()),
        check_vma=False,
    )
```

```python
import functools

import jax
import jax.numpy as jnp
from jax import lax
from jax.experimental import pallas as pl
from jax.experimental.pallas import tpu as pltpu
from jax.sharding import Mesh
from jax.sharding import PartitionSpec as P


LON = ("lon_0", "lon_1", "lon_2")
TM = ("tm_0", "tm_1")
TM_LON = TM + LON
C = 80
F = 256
LAT = 64
BAND = 8
HALO = 4
OBS = 256
W2 = 2 * LAT
F32 = jnp.float32
BF16 = jnp.bfloat16
KC = 0.7978845608028654


def lanes(rows=C):
    return lax.broadcasted_iota(jnp.int32, (rows, W2), 1)


def call(kernel, ins, outs, scratch=(), limit=8, scalars=0):
    smem = pl.BlockSpec(memory_space=pltpu.SMEM)
    vmem = pl.BlockSpec(memory_space=pltpu.VMEM)
    return pl.pallas_call(
        kernel,
        out_shape=tuple(jax.ShapeDtypeStruct(shape, dtype) for shape, dtype in outs),
        in_specs=[smem] * scalars + [vmem] * (len(ins) - scalars),
        out_specs=tuple(vmem for _ in outs),
        scratch_shapes=list(scratch),
        compiler_params=pltpu.CompilerParams(vmem_limit_bytes=limit << 20),
    )(*ins)


def dot(a, b):
    return jnp.dot(a, b, preferred_element_type=F32)


def earlier_lat(v):
    lane = lanes(v.shape[0])
    return jnp.where((lane == 0) | (lane == LAT), 0.0, pltpu.roll(v, 1, 1))


def later_lat(v):
    lane = lanes(v.shape[0])
    return jnp.where((lane == LAT - 1) | (lane == W2 - 1), 0.0, pltpu.roll(v, W2 - 1, 1))


def halves(v):
    return pltpu.roll(v, LAT, 1)


def pack_kernel(place_ref, step_ref, x_ref, xp_ref, xl_ref, xr_ref, place_row, step_row):
    place_row[...] = jnp.full((1, W2), place_ref[0], jnp.int32)
    step_row[...] = jnp.full((1, W2), step_ref[0], F32)
    for i in range(BAND):
        v = jnp.concatenate([x_ref[0, i], x_ref[1, i]], axis=0).T
        xp_ref[i] = v
        half = xl_ref if i < HALO else xr_ref
        half[i % HALO] = v.astype(BF16)


def pack(place, step, x):
    edge = ((HALO, C, W2), BF16)
    outs = [((BAND, C, W2), F32), edge, edge, ((1, W2), jnp.int32), ((1, W2), F32)]
    return call(pack_kernel, [place, step, x], outs, scalars=2)


def weights_kernel(ot_ref, c_ref, b1_ref, b2_ref, mw_ref, bw_ref, bg_ref,
                   o_ref, k2_ref, wia_ref, woa_ref, bias_ref, small_ref, bgp_ref, tall, row):
    tall[9 * C :, :] = jnp.zeros((768 - 9 * C, F), F32)
    tall[: 9 * C, :] = ot_ref[...].astype(F32)
    o_ref[...] = tall[...].T[:, : 9 * C].astype(BF16)
    turned = ot_ref
    for t in range(9):
        a, b = divmod(t, 3)
        block = c_ref[:, F * t : F * (t + 1)]
        k2_ref[C * b : C * (b + 1), F * a : F * (a + 1)] = block
        tall[C * (8 - t) : C * (9 - t), :] = block.astype(F32)
        wia_ref[C * b : C * (b + 1), F * a : F * (a + 1)] = turned[C * (8 - t) : C * (9 - t), :]
    back = tall[...].T
    woa_ref[...] = back[:, : 9 * C].astype(BF16)
    bias_ref[...] = jnp.broadcast_to(b1_ref[...], (W2, F)).T
    row[...] = jnp.zeros((W2, W2), F32)
    for n, ref in enumerate((b2_ref, mw_ref, bw_ref)):
        row[:, :C] = jnp.broadcast_to(ref[...], (W2, C))
        small_ref[n] = row[...].T[:C]
    for i in range(BAND):
        bgp_ref[i] = jnp.concatenate([bg_ref[i], jnp.zeros((LAT, C), F32)], axis=0).T


def prepare_weights(opening_t, closing, b1, b2, mw, bw, bg):
    ins = [opening_t, closing, b1[None], b2[None], mw[None], bw[None], bg]
    outs = [((F, 9 * C), BF16), ((3 * C, 3 * F), BF16), ((3 * C, 3 * F), BF16), ((F, 9 * C), BF16)]
    outs += [((F, W2), F32), ((3, C, W2), F32), ((BAND, C, W2), F32)]
    return call(
        weights_kernel,
        ins,
        outs,
        [pltpu.VMEM((768, F), F32), pltpu.VMEM((W2, W2), F32)],
    )


def split3(v):
    hi = v.astype(BF16)
    rest = v - hi.astype(F32)
    mid = rest.astype(BF16)
    low = (rest - mid.astype(F32)).astype(BF16)
    return jnp.concatenate([hi, mid, low], axis=0)


def join3(v):
    return (v[2 * C :] + v[C : 2 * C]) + v[:C]


def obs_kernel(cell_ref, chan_ref, val_ref, wt_ref, x_ref, r_ref, s_ref, hot, plain=False):
    def line(ref):
        return jnp.concatenate([ref[0:1, :], ref[1:2, :]], axis=1)

    cell = line(cell_ref)
    sub = (lax.broadcasted_iota(jnp.int32, cell.shape, 1) >= OBS).astype(jnp.int32)
    spot = (cell >> 6) * W2 + sub * LAT + (cell & (LAT - 1))
    rows = 2 * W2
    for p in range(BAND // 2):
        at = lax.broadcasted_iota(jnp.int32, (rows, 2 * OBS), 0) + p * rows
        hot[p] = jnp.where(at == spot, 1.0, 0.0).astype(BF16)
    total = jnp.zeros((3 * C, 2 * OBS), F32)
    for p in range(BAND // 2):
        total = total + dot(split3(jnp.concatenate([x_ref[2 * p], x_ref[2 * p + 1]], axis=1)), hot[p])
    mine = lax.broadcasted_iota(jnp.int32, (C, 2 * OBS), 0) == line(chan_ref)
    r = jnp.sum(jnp.where(mine, join3(total), 0.0), axis=0, keepdims=True)
    if not plain:
        r = r - line(val_ref)
    r_ref[0:1, :] = r[:, :OBS]
    r_ref[1:2, :] = r[:, OBS:]
    spread = split3(jnp.where(mine, line(wt_ref) * r, 0.0))
    for p in range(BAND // 2):
        got = lax.dot_general(spread, hot[p], (((1,), (1,)), ((), ())), preferred_element_type=F32)
        got = join3(got)
        s_ref[2 * p] = got[:, :W2]
        s_ref[2 * p + 1] = got[:, W2:]


def observe(cell, chan, val, wt, field, plain):
    return call(
        functools.partial(obs_kernel, plain=plain),
        [cell, chan, val, wt, field],
        [((2, OBS), F32), ((BAND, C, W2), F32)],
        [pltpu.VMEM((BAND // 2, 2 * W2, 2 * OBS), BF16)],
    )


def strip_kernel(l_ref, a_ref, b_ref, r_ref, up_ref, down_ref):
    def at(e):
        if e < 0:
            return l_ref[HALO + e].astype(F32)
        if e < HALO:
            return a_ref[e].astype(F32)
        if e < BAND:
            return b_ref[e - HALO].astype(F32)
        return r_ref[e - BAND].astype(F32)

    left = lanes() < LAT
    for p in range(6):
        one, two = at(p - 2), at(p + 4)
        up_ref[p] = jnp.where(left, one, halves(two)).astype(BF16)
        down_ref[p] = jnp.where(left, halves(one), two).astype(BF16)


def strips(from_left, mine_left, mine_right, from_right):
    strip = ((6, C, W2), BF16)
    return call(strip_kernel, [from_left, mine_left, mine_right, from_right], [strip, strip])


def gelu_pair(v):
    sq = v * v
    t = jnp.tanh(v * (KC + (KC * 0.044715) * sq))
    half = 0.5 * (1.0 + t)
    slope = half + (0.5 * v) * (1.0 - t * t) * (KC + (3 * KC * 0.044715) * sq)
    return v * half, slope


def stack_lats(ref, n, v):
    ref[3 * C * n : 3 * C * n + C] = earlier_lat(v).astype(BF16)
    ref[3 * C * n + C : 3 * C * n + 2 * C] = v.astype(BF16)
    ref[3 * C * n + 2 * C : 3 * C * n + 3 * C] = later_lat(v).astype(BF16)


def window(ref, n, rows):
    return jnp.concatenate([ref[rows * n : rows * (n + 3)], ref[rows * (n + 1) : rows * (n + 4)]], axis=1)


def sum_lats(s):
    res = []
    for k in range(2):
        part = s[:, W2 * k : W2 * (k + 1)]
        res.append(earlier_lat(part[:C]) + part[C : 2 * C] + later_lat(part[2 * C :]))
    return res


def step_from(sums, step, total):
    whole = jnp.sum(sums, axis=0, keepdims=True)
    lane = lax.broadcasted_iota(jnp.int32, whole.shape, 1)
    norm = jnp.sum(jnp.where(lane == 0, whole, 0.0), axis=1, keepdims=True)
    return step[:, :1] / jnp.sqrt(norm / total + 1e-06)


def gradient_kernel(total, second, n_tm, n_all):
    def kernel(*refs):
        refs = list(refs)
        take = lambda n: [refs.pop(0) for _ in range(n)]
        (place_ref,) = take(1)
        if second:
            step_ref, sums_ref = take(2)
            g0_ref, glft, grgt, upp1, dwn1, r1_ref, s1_ref = take(7)
        own_ref, lft, rgt, upp0, dwn0, r0_ref, s0_ref = take(7)
        bg_ref, wt_ref, o_ref, k2_ref, wia_ref, woa_ref, bias_ref, small_ref = take(8)
        if second:
            g_ref, x1_ref, row_ref = take(3)
        else:
            g_ref, gl_ref, gr_ref, row_ref = take(4)
        vx, hid, slope, vl, x_ext, x_prev, ln, gh = refs
        place = place_ref[...]
        left = lanes() < LAT
        if second:
            alpha = step_from(sums_ref[...], step_ref[...], total)

            def upp(n):
                return upp0[n].astype(F32) - alpha * upp1[n].astype(F32)

            def dwn(n):
                return dwn0[n].astype(F32) - alpha * dwn1[n].astype(F32)

            def obs(n):
                return s0_ref[n] - alpha * s1_ref[n]

            for e in range(16):
                v = lft[e] if e < HALO else own_ref[e - HALO] if e < HALO + BAND else rgt[e - HALO - BAND]
                g = glft[e] if e < HALO else g0_ref[e - HALO] if e < HALO + BAND else grgt[e - HALO - BAND]
                v = v.astype(F32) - alpha * g.astype(F32)
                x_ext[e] = v
                if HALO <= e < HALO + BAND:
                    x1_ref[e - HALO] = v
                stack_lats(vx, e, v)
        else:

            def upp(n):
                return upp0[n].astype(F32)

            def dwn(n):
                return dwn0[n].astype(F32)

            def obs(n):
                return s0_ref[n]

            for e in range(16):
                v = lft[e] if e < HALO else own_ref[e - HALO] if e < HALO + BAND else rgt[e - HALO - BAND]
                v = v.astype(F32)
                x_ext[e] = v
                stack_lats(vx, e, v)
        bias = bias_ref[...]
        bias2 = jnp.concatenate([bias, bias], axis=1)
        b2 = small_ref[0]
        mw = small_ref[1]
        bw = small_ref[2]
        for h in range(0, 14, 2):
            pre = dot(o_ref[...], window(vx, h, 3 * C)) + bias2
            act, sl = gelu_pair(pre)
            for k in range(2):
                n = h + k
                hid[F * n : F * (n + 1)] = act[:, W2 * k : W2 * (k + 1)].astype(BF16)
                if 2 <= n < 12:
                    slope[n - 2] = sl[:, W2 * k : W2 * (k + 1)]
        for o in range(0, 12, 2):
            s = sum_lats(dot(k2_ref[...], window(hid, o, F)))
            for k in range(2):
                n = o + k
                x = x_ext[n + 2]
                m = x + s[k] + b2
                u = upp(n % 6)
                nxt = jnp.where(left, halves(x), u if n >= 6 else halves(u))
                keep = left | (place < n_tm - 1)
                lv = jnp.where(keep, mw * (nxt - m), 0.0)
                ln[n] = lv
                stack_lats(vl, n, lv)
        for h in range(0, 10, 2):
            z = dot(woa_ref[...], window(vl, h, 3 * C))
            for k in range(2):
                n = h + k
                hid[F * n : F * (n + 1)] = (slope[n] * z[:, W2 * k : W2 * (k + 1)]).astype(BF16)
        for o in range(0, BAND, 2):
            s = sum_lats(dot(wia_ref[...], window(hid, o, F)))
            for k in range(2):
                gh[o + k] = ln[o + k + 2] + s[k]
        for r in range(8):
            one = dwn(r) if r < 6 else halves(dwn(r - 6))
            two = dwn(r - 2) if r >= 2 else halves(dwn(r + 4))
            v = jnp.where(left, one, two)
            x_prev[r] = v
            stack_lats(vx, r, v)
        for h in range(0, 6, 2):
            act, _ = gelu_pair(dot(o_ref[...], window(vx, h, 3 * C)) + bias2)
            for k in range(2):
                n = h + k
                hid[F * n : F * (n + 1)] = act[:, W2 * k : W2 * (k + 1)].astype(BF16)
        squares = jnp.zeros((C, W2), F32)
        cost = jnp.zeros((C, W2), F32)
        for o in range(0, 4, 2):
            s = sum_lats(dot(k2_ref[...], window(hid, o, F)))
            for k in range(2):
                m = x_prev[o + k + 2] + s[k] + b2
                for side in range(2):
                    i = o + k + 4 * side
                    x = x_ext[i + HALO]
                    before = m if side == 0 else halves(m)
                    first = jnp.where(place > 0, mw * (x - before), 0.0)
                    lo = jnp.where(left, first, halves(ln[i + 2]))
                    dep = jnp.where(left & (place == 0), x - bg_ref[i], 0.0)
                    g = lo - gh[i] + obs(i) + bw * dep
                    g_ref[i] = g
                    if not second:
                        edge = gl_ref if i < HALO else gr_ref
                        edge[i % HALO] = g.astype(BF16)
                    squares = squares + g * g
                    cost = cost + lo * lo / mw + bw * dep * dep
        r = r0_ref[...]
        if second:
            r = r - alpha * r1_ref[...]
        paid = jnp.sum(jnp.sum(wt_ref[...] * r * r, axis=0, keepdims=True), axis=1, keepdims=True)
        norm = jnp.sum(jnp.sum(squares, axis=0, keepdims=True), axis=1, keepdims=True)
        paid = 0.5 * (paid + jnp.sum(jnp.sum(cost, axis=0, keepdims=True), axis=1, keepdims=True))
        lane = lax.broadcasted_iota(jnp.int32, (n_all, W2), 1)
        row_ref[...] = jnp.where(lane == 0, norm, jnp.where(lane == 1, paid, 0.0))

    return kernel


def gradient(total, n_tm, n_all, ins, second):
    full = ((BAND, C, W2), F32)
    edge = ((HALO, C, W2), BF16)
    row = ((n_all, W2), F32)
    outs = [full, full, row] if second else [full, edge, edge, row]
    return call(
        gradient_kernel(total, second, n_tm, n_all),
        ins,
        outs,
        [
            pltpu.VMEM((16 * 3 * C, W2), BF16),
            pltpu.VMEM((14 * F, W2), BF16),
            pltpu.VMEM((10, F, W2), F32),
            pltpu.VMEM((12 * 3 * C, W2), BF16),
            pltpu.VMEM((16, C, W2), F32),
            pltpu.VMEM((8, C, W2), F32),
            pltpu.VMEM((12, C, W2), F32),
            pltpu.VMEM((BAND, C, W2), F32),
        ],
        limit=24,
    )


def final_kernel(total):
    def kernel(step_ref, first_ref, sums_ref, x_ref, g_ref, x_out, cost_out):
        alpha = step_from(sums_ref[...], step_ref[...], total)
        for i in range(BAND):
            v = x_ref[i] - alpha * g_ref[i]
            v = jnp.concatenate([v, jnp.zeros((W2 - C, W2), F32)], axis=0).T[:, :C]
            x_out[0, i] = v[:LAT]
            x_out[1, i] = v[LAT:]
        c0 = jnp.sum(first_ref[...], axis=0, keepdims=True)
        c1 = jnp.sum(sums_ref[...], axis=0, keepdims=True)
        lane = lax.broadcasted_iota(jnp.int32, c0.shape, 1)
        one = jnp.sum(jnp.where(lane == 1, c0, 0.0), axis=1, keepdims=True)
        two = jnp.sum(jnp.where(lane == 1, c1, 0.0), axis=1, keepdims=True)
        cost_out[...] = jnp.where(lane == 0, one, two)[:, :2]

    return kernel


def shifted(value, axes, by, closed):
    n = lax.axis_size(axes)
    pairs = [(i, (i + by) % n) for i in range(n) if closed or 0 <= i + by < n]
    return lax.ppermute(value, axes, pairs)


def exchange(mine_left, mine_right):
    from_right = shifted(mine_left, LON, -1, True)
    from_left = shifted(mine_right, LON, 1, True)
    up, down = strips(from_left, mine_left, mine_right, from_right)
    after = shifted(up, TM, -1, False)
    before = shifted(down, TM, 1, False)
    return (from_left, from_right, after, before), up


def per_device(x, background, opening, b1, closing, b2, mw, bw, cell, chan, val, wt, step):
    n_tm = lax.axis_size(TM)
    n_all = n_tm * lax.axis_size(LON)
    total = float(2 * BAND * C * LAT * n_all)
    place = lax.axis_index(TM).astype(jnp.int32)[None]
    step = step[None]
    xp, xl, xr, place, step = pack(place, step, jnp.swapaxes(x, 2, 3))
    halo, _ = exchange(xl, xr)
    o, k2, wia, woa, bias, small, bgp = prepare_weights(
        opening.T, closing, b1, b2, mw, bw, jnp.swapaxes(background, 1, 2)
    )
    r0, s0 = observe(cell, chan, val, wt, xp, False)
    consts = (bgp, wt, o, k2, wia, woa, bias, small)
    base = (xp,) + halo + (r0, s0)
    g0, gl, gr, row = gradient(total, n_tm, n_all, (place,) + base + consts, False)
    sums0 = lax.all_to_all(row, TM_LON, 0, 0, tiled=True)
    ghalo, up = exchange(gl, gr)
    later_g0, _ = lax.optimization_barrier((g0, up))
    rg, sg = observe(cell, chan, val, wt, later_g0, True)
    ins = (place, step, sums0, g0) + ghalo + (rg, sg) + base + consts
    g1, x1, row = gradient(total, n_tm, n_all, ins, True)
    sums1 = lax.all_to_all(row, TM_LON, 0, 0, tiled=True)
    x2, costs = call(
        final_kernel(total),
        [step, sums0, sums1, x1, g1],
        [((2, BAND, LAT, C), F32), ((1, 2), F32)],
    )
    return jnp.swapaxes(x2, 2, 3), costs.reshape(2)


def solution(mesh):
    n_tm, n_lon = mesh.devices.shape
    if (n_tm, n_lon) == (8, 32):
        shape = (4, 2, 2, 8, 2)
    else:
        shape = (n_tm, 1, 1, n_lon // 2, 2)
    split = Mesh(mesh.devices.reshape(shape), TM_LON)
    placed = (
        P(TM, LON, None, None),
        P(LON, None, None),
        P(), P(), P(), P(), P(), P(),
        P(TM, LON), P(TM, LON), P(TM, LON), P(TM, LON),
        P(),
    )
    return jax.shard_map(
        per_device,
        mesh=split,
        in_specs=placed,
        out_specs=(P(TM, LON, None, None), P()),
        check_vma=False,
    )
```

```python
import functools

import jax
import jax.numpy as jnp
from jax import lax
from jax.experimental import pallas as pl
from jax.experimental.pallas import tpu as pltpu
from jax.sharding import Mesh
from jax.sharding import PartitionSpec as P


LON = ("lon_0", "lon_1", "lon_2")
TM = ("tm_0", "tm_1")
TM_LON = TM + LON
C = 80
F = 256
LAT = 64
BAND = 8
HALO = 4
OBS = 256
W2 = 2 * LAT
F32 = jnp.float32
BF16 = jnp.bfloat16
KC = 0.7978845608028654


def lanes(rows=C):
    return lax.broadcasted_iota(jnp.int32, (rows, W2), 1)


def call(kernel, ins, outs, scratch=(), limit=8, scalars=0):
    smem = pl.BlockSpec(memory_space=pltpu.SMEM)
    vmem = pl.BlockSpec(memory_space=pltpu.VMEM)
    return pl.pallas_call(
        kernel,
        out_shape=tuple(jax.ShapeDtypeStruct(shape, dtype) for shape, dtype in outs),
        in_specs=[smem] * scalars + [vmem] * (len(ins) - scalars),
        out_specs=tuple(vmem for _ in outs),
        scratch_shapes=list(scratch),
        compiler_params=pltpu.CompilerParams(vmem_limit_bytes=limit << 20),
    )(*ins)


def dot(a, b):
    return jnp.dot(a, b, preferred_element_type=F32)


def earlier_lat(v):
    lane = lanes(v.shape[0])
    return jnp.where((lane == 0) | (lane == LAT), 0.0, pltpu.roll(v, 1, 1))


def later_lat(v):
    lane = lanes(v.shape[0])
    return jnp.where((lane == LAT - 1) | (lane == W2 - 1), 0.0, pltpu.roll(v, W2 - 1, 1))


def halves(v):
    return pltpu.roll(v, LAT, 1)


def pack_kernel(place_ref, step_ref, x_ref, xp_ref, xl_ref, xr_ref, place_row, step_row):
    place_row[...] = jnp.full((1, W2), place_ref[0], jnp.int32)
    step_row[...] = jnp.full((1, W2), step_ref[0], F32)
    for i in range(BAND):
        v = jnp.concatenate([x_ref[0, i], x_ref[1, i]], axis=0).T
        xp_ref[i] = v
        half = xl_ref if i < HALO else xr_ref
        half[i % HALO] = v.astype(BF16)


def pack(place, step, x):
    edge = ((HALO, C, W2), BF16)
    outs = [((BAND, C, W2), F32), edge, edge, ((1, W2), jnp.int32), ((1, W2), F32)]
    return call(pack_kernel, [place, step, x], outs, scalars=2)


def weights_kernel(ot_ref, c_ref, b1_ref, b2_ref, mw_ref, bw_ref, bg_ref,
                   o_ref, k2_ref, wia_ref, woa_ref, bias_ref, small_ref, bgp_ref, tall, row):
    tall[9 * C :, :] = jnp.zeros((768 - 9 * C, F), F32)
    tall[: 9 * C, :] = ot_ref[...].astype(F32)
    o_ref[...] = tall[...].T[:, : 9 * C].astype(BF16)
    turned = ot_ref
    for t in range(9):
        a, b = divmod(t, 3)
        block = c_ref[:, F * t : F * (t + 1)]
        k2_ref[C * b : C * (b + 1), F * a : F * (a + 1)] = block
        tall[C * (8 - t) : C * (9 - t), :] = block.astype(F32)
        wia_ref[C * b : C * (b + 1), F * a : F * (a + 1)] = turned[C * (8 - t) : C * (9 - t), :]
    back = tall[...].T
    woa_ref[...] = back[:, : 9 * C].astype(BF16)
    bias_ref[...] = jnp.broadcast_to(b1_ref[...], (W2, F)).T
    row[...] = jnp.zeros((W2, W2), F32)
    for n, ref in enumerate((b2_ref, mw_ref, bw_ref)):
        row[:, :C] = jnp.broadcast_to(ref[...], (W2, C))
        small_ref[n] = row[...].T[:C]
    for i in range(BAND):
        bgp_ref[i] = jnp.concatenate([bg_ref[i], jnp.zeros((LAT, C), F32)], axis=0).T


def prepare_weights(opening_t, closing, b1, b2, mw, bw, bg):
    ins = [opening_t, closing, b1[None], b2[None], mw[None], bw[None], bg]
    outs = [((F, 9 * C), BF16), ((3 * C, 3 * F), BF16), ((3 * C, 3 * F), BF16), ((F, 9 * C), BF16)]
    outs += [((F, W2), F32), ((3, C, W2), F32), ((BAND, C, W2), F32)]
    return call(
        weights_kernel,
        ins,
        outs,
        [pltpu.VMEM((768, F), F32), pltpu.VMEM((W2, W2), F32)],
    )


def split3(v):
    hi = v.astype(BF16)
    rest = v - hi.astype(F32)
    mid = rest.astype(BF16)
    low = (rest - mid.astype(F32)).astype(BF16)
    return jnp.concatenate([hi, mid, low], axis=0)


def join3(v):
    return (v[2 * C :] + v[C : 2 * C]) + v[:C]


def obs_kernel(cell_ref, chan_ref, val_ref, wt_ref, x_ref, r_ref, s_ref, hot, plain=False):
    def line(ref):
        return jnp.concatenate([ref[0:1, :], ref[1:2, :]], axis=1)

    cell = line(cell_ref)
    sub = (lax.broadcasted_iota(jnp.int32, cell.shape, 1) >= OBS).astype(jnp.int32)
    spot = (cell >> 6) * W2 + sub * LAT + (cell & (LAT - 1))
    rows = 2 * W2
    for p in range(BAND // 2):
        at = lax.broadcasted_iota(jnp.int32, (rows, 2 * OBS), 0) + p * rows
        hot[p] = jnp.where(at == spot, 1.0, 0.0).astype(BF16)
    total = jnp.zeros((3 * C, 2 * OBS), F32)
    for p in range(BAND // 2):
        total = total + dot(split3(jnp.concatenate([x_ref[2 * p], x_ref[2 * p + 1]], axis=1)), hot[p])
    mine = lax.broadcasted_iota(jnp.int32, (C, 2 * OBS), 0) == line(chan_ref)
    r = jnp.sum(jnp.where(mine, join3(total), 0.0), axis=0, keepdims=True)
    if not plain:
        r = r - line(val_ref)
    r_ref[0:1, :] = r[:, :OBS]
    r_ref[1:2, :] = r[:, OBS:]
    spread = split3(jnp.where(mine, line(wt_ref) * r, 0.0))
    for p in range(BAND // 2):
        got = lax.dot_general(spread, hot[p], (((1,), (1,)), ((), ())), preferred_element_type=F32)
        got = join3(got)
        s_ref[2 * p] = got[:, :W2]
        s_ref[2 * p + 1] = got[:, W2:]


def observe(cell, chan, val, wt, field, plain):
    return call(
        functools.partial(obs_kernel, plain=plain),
        [cell, chan, val, wt, field],
        [((2, OBS), F32), ((BAND, C, W2), F32)],
        [pltpu.VMEM((BAND // 2, 2 * W2, 2 * OBS), BF16)],
    )


def strip_kernel(l_ref, a_ref, b_ref, r_ref, up_ref, down_ref):
    def at(e):
        if e < 0:
            return l_ref[HALO + e].astype(F32)
        if e < HALO:
            return a_ref[e].astype(F32)
        if e < BAND:
            return b_ref[e - HALO].astype(F32)
        return r_ref[e - BAND].astype(F32)

    left = lanes() < LAT
    for p in range(6):
        one, two = at(p - 2), at(p + 4)
        up_ref[p] = jnp.where(left, one, halves(two)).astype(BF16)
        down_ref[p] = jnp.where(left, halves(one), two).astype(BF16)


def strips(from_left, mine_left, mine_right, from_right):
    strip = ((6, C, W2), BF16)
    return call(strip_kernel, [from_left, mine_left, mine_right, from_right], [strip, strip])


def gelu_pair(v):
    sq = v * v
    t = jnp.tanh(v * (KC + (KC * 0.044715) * sq))
    half = 0.5 * (1.0 + t)
    slope = half + (0.5 * v) * (1.0 - t * t) * (KC + (3 * KC * 0.044715) * sq)
    return v * half, slope


def stack_lats(ref, n, v):
    ref[3 * C * n : 3 * C * n + C] = earlier_lat(v).astype(BF16)
    ref[3 * C * n + C : 3 * C * n + 2 * C] = v.astype(BF16)
    ref[3 * C * n + 2 * C : 3 * C * n + 3 * C] = later_lat(v).astype(BF16)


def window(ref, n, rows):
    return jnp.concatenate([ref[rows * n : rows * (n + 3)], ref[rows * (n + 1) : rows * (n + 4)]], axis=1)


def sum_lats(s):
    res = []
    for k in range(2):
        part = s[:, W2 * k : W2 * (k + 1)]
        res.append(earlier_lat(part[:C]) + part[C : 2 * C] + later_lat(part[2 * C :]))
    return res


def step_from(sums, step, total):
    whole = jnp.sum(sums, axis=0, keepdims=True)
    lane = lax.broadcasted_iota(jnp.int32, whole.shape, 1)
    norm = jnp.sum(jnp.where(lane == 0, whole, 0.0), axis=1, keepdims=True)
    return step[:, :1] / jnp.sqrt(norm / total + 1e-06)


def forward_kernel(total, second):
    def kernel(*refs):
        refs = list(refs)
        take = lambda n: [refs.pop(0) for _ in range(n)]
        if second:
            step_ref, sums_ref, g0_ref, glft, grgt = take(5)
        own_ref, lft, rgt, o_ref, k2_ref, bias_ref, small_ref = take(7)
        x_ref, m_ref, slope = take(3)
        alpha_ref = take(1)[0] if second else None
        vx, hid = refs
        if second:
            alpha = step_from(sums_ref[...], step_ref[...], total)
            alpha_ref[...] = jnp.broadcast_to(alpha, (1, W2))

        def pick(e, one, two, three):
            return one[e] if e < HALO else two[e - HALO] if e < HALO + BAND else three[e - HALO - BAND]

        for e in range(16):
            v = pick(e, lft, own_ref, rgt).astype(F32)
            if second:
                v = v - alpha * pick(e, glft, g0_ref, grgt).astype(F32)
            if 2 <= e < 14:
                x_ref[e - 2] = v
            stack_lats(vx, e, v)
        bias = bias_ref[...]
        bias2 = jnp.concatenate([bias, bias], axis=1)
        for h in range(0, 14, 2):
            pre = dot(o_ref[...], window(vx, h, 3 * C)) + bias2
            act, sl = gelu_pair(pre)
            for k in range(2):
                n = h + k
                hid[F * n : F * (n + 1)] = act[:, W2 * k : W2 * (k + 1)].astype(BF16)
                if 2 <= n < 12:
                    slope[n - 2] = sl[:, W2 * k : W2 * (k + 1)]
        for o in range(0, 12, 2):
            s = sum_lats(dot(k2_ref[...], window(hid, o, F)))
            for k in range(2):
                m_ref[o + k] = x_ref[o + k] + s[k] + small_ref[0]

    return kernel


def forward(total, ins, second):
    outs = [((12, C, W2), F32), ((12, C, W2), F32), ((10, F, W2), F32)] + ([((1, W2), F32)] if second else [])
    scratch = [pltpu.VMEM((16 * 3 * C, W2), BF16), pltpu.VMEM((14 * F, W2), BF16)]
    return call(forward_kernel(total, second), ins, outs, scratch, limit=16)


def adjoint_kernel(second, n_tm):
    def kernel(*refs):
        refs = list(refs)
        take = lambda n: [refs.pop(0) for _ in range(n)]
        place_ref, x_ref, m_ref, slope, upp0 = take(5)
        alpha_ref, upp1 = take(2) if second else (None, None)
        woa_ref, wia_ref, small_ref = take(3)
        pulled, held, vl, hid, ln = refs
        place = place_ref[...]
        left = lanes() < LAT
        keep = left | (place < n_tm - 1)
        for n in range(12):
            u = upp0[n % 6].astype(F32)
            if second:
                u = u - alpha_ref[...] * upp1[n % 6].astype(F32)
            nxt = jnp.where(left, halves(x_ref[n]), u if n >= 6 else halves(u))
            lv = jnp.where(keep, small_ref[1] * (nxt - m_ref[n]), 0.0)
            if 2 <= n < 10:
                ln[n - 2] = lv
                held[n - 2] = halves(lv)
            stack_lats(vl, n, lv)
        for h in range(0, 10, 2):
            z = dot(woa_ref[...], window(vl, h, 3 * C))
            for k in range(2):
                n = h + k
                hid[F * n : F * (n + 1)] = (slope[n] * z[:, W2 * k : W2 * (k + 1)]).astype(BF16)
        for o in range(0, BAND, 2):
            s = sum_lats(dot(wia_ref[...], window(hid, o, F)))
            for k in range(2):
                pulled[o + k] = ln[o + k] + s[k]

    return kernel


def adjoint(n_tm, ins, second):
    full = ((BAND, C, W2), F32)
    scratch = [pltpu.VMEM((12 * 3 * C, W2), BF16), pltpu.VMEM((10 * F, W2), BF16), pltpu.VMEM((BAND, C, W2), F32)]
    return call(adjoint_kernel(second, n_tm), ins, [full, full], scratch, limit=16)


def gradient_kernel(second, n_all):
    def kernel(*refs):
        refs = list(refs)
        take = lambda n: [refs.pop(0) for _ in range(n)]
        place_ref, x_ref, pulled, held, dwn0, r0_ref, s0_ref = take(7)
        if second:
            alpha_ref, dwn1, r1_ref, s1_ref = take(4)
        bg_ref, wt_ref, o_ref, k2_ref, bias_ref, small_ref = take(6)
        g_ref, row_ref = take(2)
        gl_ref, gr_ref = (None, None) if second else take(2)
        vx, hid, x_prev = refs
        place = place_ref[...]
        left = lanes() < LAT
        b2, mw, bw = small_ref[0], small_ref[1], small_ref[2]

        def dwn(n):
            v = dwn0[n].astype(F32)
            return v - alpha_ref[...] * dwn1[n].astype(F32) if second else v

        for r in range(8):
            one = dwn(r) if r < 6 else halves(dwn(r - 6))
            two = dwn(r - 2) if r >= 2 else halves(dwn(r + 4))
            v = jnp.where(left, one, two)
            x_prev[r] = v
            stack_lats(vx, r, v)
        bias = bias_ref[...]
        bias2 = jnp.concatenate([bias, bias], axis=1)
        for h in range(0, 6, 2):
            act, _ = gelu_pair(dot(o_ref[...], window(vx, h, 3 * C)) + bias2)
            for k in range(2):
                n = h + k
                hid[F * n : F * (n + 1)] = act[:, W2 * k : W2 * (k + 1)].astype(BF16)
        squares = jnp.zeros((C, W2), F32)
        cost = jnp.zeros((C, W2), F32)
        for o in range(0, 4, 2):
            s = sum_lats(dot(k2_ref[...], window(hid, o, F)))
            for k in range(2):
                m = x_prev[o + k + 2] + s[k] + b2
                for side in range(2):
                    i = o + k + 4 * side
                    x = x_ref[i + 2]
                    before = m if side == 0 else halves(m)
                    first = jnp.where(place > 0, mw * (x - before), 0.0)
                    lo = jnp.where(left, first, held[i])
                    dep = jnp.where(left & (place == 0), x - bg_ref[i], 0.0)
                    seen = s0_ref[i]
                    if second:
                        seen = seen - alpha_ref[...] * s1_ref[i]
                    g = lo - pulled[i] + seen + bw * dep
                    g_ref[i] = g
                    if not second:
                        edge = gl_ref if i < HALO else gr_ref
                        edge[i % HALO] = g.astype(BF16)
                    squares = squares + g * g
                    cost = cost + lo * lo / mw + bw * dep * dep
        r = r0_ref[...]
        if second:
            r = r - alpha_ref[:, :1] * r1_ref[...]
        paid = jnp.sum(jnp.sum(wt_ref[...] * r * r, axis=0, keepdims=True), axis=1, keepdims=True)
        norm = jnp.sum(jnp.sum(squares, axis=0, keepdims=True), axis=1, keepdims=True)
        paid = 0.5 * (paid + jnp.sum(jnp.sum(cost, axis=0, keepdims=True), axis=1, keepdims=True))
        lane = lax.broadcasted_iota(jnp.int32, (n_all, W2), 1)
        row_ref[...] = jnp.where(lane == 0, norm, jnp.where(lane == 1, paid, 0.0))

    return kernel


def gradient(n_all, ins, second):
    edge = ((HALO, C, W2), BF16)
    outs = [((BAND, C, W2), F32), ((n_all, W2), F32)] + ([] if second else [edge, edge])
    scratch = [pltpu.VMEM((8 * 3 * C, W2), BF16), pltpu.VMEM((6 * F, W2), BF16), pltpu.VMEM((8, C, W2), F32)]
    return call(gradient_kernel(second, n_all), ins, outs, scratch, limit=16)


def final_kernel(total):
    def kernel(step_ref, first_ref, sums_ref, x_ref, g_ref, x_out, cost_out):
        alpha = step_from(sums_ref[...], step_ref[...], total)
        for i in range(BAND):
            v = x_ref[i + 2] - alpha * g_ref[i]
            v = jnp.concatenate([v, jnp.zeros((W2 - C, W2), F32)], axis=0).T[:, :C]
            x_out[0, i] = v[:LAT]
            x_out[1, i] = v[LAT:]
        c0 = jnp.sum(first_ref[...], axis=0, keepdims=True)
        c1 = jnp.sum(sums_ref[...], axis=0, keepdims=True)
        lane = lax.broadcasted_iota(jnp.int32, c0.shape, 1)
        one = jnp.sum(jnp.where(lane == 1, c0, 0.0), axis=1, keepdims=True)
        two = jnp.sum(jnp.where(lane == 1, c1, 0.0), axis=1, keepdims=True)
        cost_out[...] = jnp.where(lane == 0, one, two)[:, :2]

    return kernel


def shifted(value, axes, by, closed):
    n = lax.axis_size(axes)
    pairs = [(i, (i + by) % n) for i in range(n) if closed or 0 <= i + by < n]
    return lax.ppermute(value, axes, pairs)


def exchange(mine_left, mine_right):
    from_right = shifted(mine_left, LON, -1, True)
    from_left = shifted(mine_right, LON, 1, True)
    up, down = strips(from_left, mine_left, mine_right, from_right)
    after = shifted(up, TM, -1, False)
    before = shifted(down, TM, 1, False)
    return from_left, from_right, after, before, up


def per_device(x, background, opening, b1, closing, b2, mw, bw, cell, chan, val, wt, step):
    n_tm = lax.axis_size(TM)
    n_all = n_tm * lax.axis_size(LON)
    total = float(2 * BAND * C * LAT * n_all)
    place = lax.axis_index(TM).astype(jnp.int32)[None]
    step = step[None]
    xp, xl, xr, place, step = pack(place, step, jnp.swapaxes(x, 2, 3))
    lft, rgt, upp, dwn, _ = exchange(xl, xr)
    o, k2, wia, woa, bias, small, bgp = prepare_weights(
        opening.T, closing, b1, b2, mw, bw, jnp.swapaxes(background, 1, 2)
    )
    nets = (o, k2, bias, small)
    own = (xp, lft, rgt) + nets
    x0, m0, slope = forward(total, own, False)
    r0, s0 = observe(cell, chan, val, wt, xp, False)
    pulled, held = adjoint(n_tm, (place, x0, m0, slope, upp, woa, wia, small), False)
    rest = (bgp, wt) + nets
    g0, row, gl, gr = gradient(n_all, (place, x0, pulled, held, dwn, r0, s0) + rest, False)
    sums0 = lax.all_to_all(row, TM_LON, 0, 0, tiled=True)
    glft, grgt, gupp, gdwn, up = exchange(gl, gr)
    later_g0, _ = lax.optimization_barrier((g0, up))
    x1, m1, slope, alpha = forward(total, (step, sums0, g0, glft, grgt) + own, True)
    rg, sg = observe(cell, chan, val, wt, later_g0, True)
    pulled, held = adjoint(n_tm, (place, x1, m1, slope, upp, alpha, gupp, woa, wia, small), True)
    g1, row = gradient(n_all, (place, x1, pulled, held, dwn, r0, s0, alpha, gdwn, rg, sg) + rest, True)
    sums1 = lax.all_to_all(row, TM_LON, 0, 0, tiled=True)
    x2, costs = call(
        final_kernel(total),
        [step, sums0, sums1, x1, g1],
        [((2, BAND, LAT, C), F32), ((1, 2), F32)],
    )
    return jnp.swapaxes(x2, 2, 3), costs.reshape(2)


def solution(mesh):
    n_tm, n_lon = mesh.devices.shape
    if (n_tm, n_lon) == (8, 32):
        shape = (4, 2, 2, 8, 2)
    else:
        shape = (n_tm, 1, 1, n_lon // 2, 2)
    split = Mesh(mesh.devices.reshape(shape), TM_LON)
    placed = (
        P(TM, LON, None, None),
        P(LON, None, None),
        P(), P(), P(), P(), P(), P(),
        P(TM, LON), P(TM, LON), P(TM, LON), P(TM, LON),
        P(),
    )
    return jax.shard_map(
        per_device,
        mesh=split,
        in_specs=placed,
        out_specs=(P(TM, LON, None, None), P()),
        check_vma=False,
    )
```

```python
import jax
import jax.numpy as jnp
from jax import lax
from jax.experimental import pallas as pl
from jax.experimental.pallas import tpu as pltpu
from jax.sharding import Mesh
from jax.sharding import PartitionSpec as P


LON = ("lon_0", "lon_1", "lon_2")
TM = ("tm_0", "tm_1")
TM_LON = TM + LON
C = 80
F = 256
LAT = 64
BAND = 8
HALO = 4
OBS = 256
W2 = 2 * LAT
F32 = jnp.float32
BF16 = jnp.bfloat16
KC = 0.7978845608028654


def lanes(rows=C):
    return lax.broadcasted_iota(jnp.int32, (rows, W2), 1)


def call(kernel, ins, outs, scratch=(), limit=8, scalars=0):
    smem = pl.BlockSpec(memory_space=pltpu.SMEM)
    vmem = pl.BlockSpec(memory_space=pltpu.VMEM)
    return pl.pallas_call(
        kernel,
        out_shape=tuple(jax.ShapeDtypeStruct(shape, dtype) for shape, dtype in outs),
        in_specs=[smem] * scalars + [vmem] * (len(ins) - scalars),
        out_specs=tuple(vmem for _ in outs),
        scratch_shapes=list(scratch),
        compiler_params=pltpu.CompilerParams(vmem_limit_bytes=limit << 20),
    )(*ins)


def dot(a, b):
    return jnp.dot(a, b, preferred_element_type=F32)


def earlier_lat(v):
    lane = lanes(v.shape[0])
    return jnp.where((lane == 0) | (lane == LAT), 0.0, pltpu.roll(v, 1, 1))


def later_lat(v):
    lane = lanes(v.shape[0])
    return jnp.where((lane == LAT - 1) | (lane == W2 - 1), 0.0, pltpu.roll(v, W2 - 1, 1))


def halves(v):
    return pltpu.roll(v, LAT, 1)


def pick(even, one, two):
    return jnp.where(even, one.astype(F32), two.astype(F32))


def pack_kernel(place_ref, band_ref, step_ref, x_ref, table_ref,
                xp_ref, s0_ref, s1_ref, place_row, band_row, step_row, spot_row, chan_row, val_row, wt_row, b1_row, small_row):
    place_row[...] = jnp.full((1, W2), place_ref[0], jnp.int32)
    band_row[...] = jnp.full((1, W2), band_ref[0], jnp.int32)
    step_row[...] = jnp.full((1, W2), step_ref[0], F32)

    def line(n):
        return jnp.concatenate([table_ref[n : n + 1, :], table_ref[n + 1 : n + 2, :]], axis=1)

    cell = line(0).astype(jnp.int32)
    sub = (lax.broadcasted_iota(jnp.int32, cell.shape, 1) >= OBS).astype(jnp.int32)
    spot_row[...] = (cell >> 6) * W2 + sub * LAT + (cell & (LAT - 1))
    chan_row[...] = line(2).astype(jnp.int32)
    val_row[...] = line(4)
    wt_row[...] = line(6)
    b1_row[...] = table_ref[8:9, :]
    small_row[...] = table_ref[9:12, :C]
    even = (jnp.full((1, W2), band_ref[0], jnp.int32) & 1) == 0
    for i in range(HALO):
        one = jnp.concatenate([x_ref[0, i], x_ref[1, i]], axis=0).T
        two = jnp.concatenate([x_ref[0, i + HALO], x_ref[1, i + HALO]], axis=0).T
        xp_ref[i] = one
        xp_ref[i + HALO] = two
        s0_ref[i] = jnp.where(even, two, one).astype(BF16)
        s1_ref[i] = jnp.where(even, one, two).astype(BF16)


def pack(place, band, step, x, obs, small):
    edge = ((HALO, C, W2), BF16)
    row = lambda n, dtype: ((1, n), dtype)
    outs = [((BAND, C, W2), F32), edge, edge, row(W2, jnp.int32), row(W2, jnp.int32), row(W2, F32)]
    outs += [row(2 * OBS, jnp.int32), row(2 * OBS, jnp.int32), row(2 * OBS, F32), row(2 * OBS, F32), row(F, F32), ((3, C), F32)]
    rows = [v.astype(F32) for v in obs] + [jnp.pad(v, (0, OBS - v.shape[0]))[None] for v in small]
    return call(pack_kernel, [place, band, step, x, jnp.concatenate(rows, axis=0)], outs, scalars=3)


def weights_kernel(ot_ref, c_ref, b1_ref, row_ref, bg_ref,
                   o_ref, k2_ref, wia_ref, woa_ref, bias_ref, small_ref, bgp_ref, tall, row):
    tall[9 * C :, :] = jnp.zeros((768 - 9 * C, F), F32)
    tall[: 9 * C, :] = ot_ref[...].astype(F32)
    o_ref[...] = tall[...].T[:, : 9 * C].astype(BF16)
    turned = ot_ref
    for t in range(9):
        a, b = divmod(t, 3)
        block = c_ref[:, F * t : F * (t + 1)]
        k2_ref[C * b : C * (b + 1), F * a : F * (a + 1)] = block
        tall[C * (8 - t) : C * (9 - t), :] = block.astype(F32)
        wia_ref[C * b : C * (b + 1), F * a : F * (a + 1)] = turned[C * (8 - t) : C * (9 - t), :]
    back = tall[...].T
    woa_ref[...] = back[:, : 9 * C].astype(BF16)
    bias_ref[...] = jnp.broadcast_to(b1_ref[...], (W2, F)).T
    row[...] = jnp.zeros((W2, W2), F32)
    for n in range(3):
        row[:, :C] = jnp.broadcast_to(row_ref[n : n + 1, :], (W2, C))
        small_ref[n] = row[...].T[:C]
    for i in range(BAND):
        bgp_ref[i] = jnp.concatenate([bg_ref[i], jnp.zeros((LAT, C), F32)], axis=0).T


def prepare_weights(opening_t, closing, b1, small, bg):
    ins = [opening_t, closing, b1, small, bg]
    outs = [((F, 9 * C), BF16), ((3 * C, 3 * F), BF16), ((3 * C, 3 * F), BF16), ((F, 9 * C), BF16)]
    outs += [((F, W2), F32), ((3, C, W2), F32), ((BAND, C, W2), F32)]
    return call(
        weights_kernel,
        ins,
        outs,
        [pltpu.VMEM((768, F), F32), pltpu.VMEM((W2, W2), F32)],
    )


def split3(v):
    hi = v.astype(BF16)
    rest = v - hi.astype(F32)
    mid = rest.astype(BF16)
    low = (rest - mid.astype(F32)).astype(BF16)
    return jnp.concatenate([hi, mid, low], axis=0)


def join3(v):
    return (v[2 * C :] + v[C : 2 * C]) + v[:C]


def obs_kernel(spot_ref, chan_ref, val_ref, wt_ref, x_ref, *refs):
    first = len(refs) == 3 and refs[0].shape[0] == 1
    if first:
        r_ref, s_ref, hot = refs
        spot = spot_ref[...]
        rows = 2 * W2
        for p in range(BAND // 2):
            at = lax.broadcasted_iota(jnp.int32, (rows, 2 * OBS), 0) + p * rows
            hot[p] = jnp.where(at == spot, 1.0, 0.0).astype(BF16)
    else:
        hot, r_ref, s_ref = refs
    total = jnp.zeros((3 * C, 2 * OBS), F32)
    for p in range(BAND // 2):
        total = total + dot(split3(jnp.concatenate([x_ref[2 * p], x_ref[2 * p + 1]], axis=1)), hot[p])
    mine = lax.broadcasted_iota(jnp.int32, (C, 2 * OBS), 0) == chan_ref[...]
    r = jnp.sum(jnp.where(mine, join3(total), 0.0), axis=0, keepdims=True)
    if first:
        r = r - val_ref[...]
    r_ref[...] = r
    spread = split3(jnp.where(mine, wt_ref[...] * r, 0.0))
    for p in range(BAND // 2):
        got = lax.dot_general(spread, hot[p], (((1,), (1,)), ((), ())), preferred_element_type=F32)
        got = join3(got)
        s_ref[2 * p] = got[:, :W2]
        s_ref[2 * p + 1] = got[:, W2:]


def observe(lines, field, hot=None):
    outs = [((1, 2 * OBS), F32), ((BAND, C, W2), F32)]
    if hot is None:
        return call(obs_kernel, list(lines) + [field], outs + [((BAND // 2, 2 * W2, 2 * OBS), BF16)])
    return call(obs_kernel, list(lines) + [field, hot], outs)


def strip_kernel(place_ref, band_ref, mine0, mine1, got0, got1, send0, send1):
    even = (band_ref[...] & 1) == 0
    even_tm = (place_ref[...] & 1) == 0

    def at(e):
        if e < 0:
            return pick(even, got1[HALO + e], got0[HALO + e])
        if e < HALO:
            return pick(even, mine1[e], mine0[e])
        if e < BAND:
            return pick(even, mine0[e - HALO], mine1[e - HALO])
        return pick(even, got0[e - BAND], got1[e - BAND])

    left = lanes() < LAT
    for p in range(6):
        one, two = at(p - 2), at(p + 4)
        up = jnp.where(left, one, halves(two))
        down = jnp.where(left, halves(one), two)
        send0[p] = jnp.where(even_tm, down, up).astype(BF16)
        send1[p] = jnp.where(even_tm, up, down).astype(BF16)


def strips(*args):
    strip = ((6, C, W2), BF16)
    return call(strip_kernel, list(args), [strip, strip])


def gelu_pair(v):
    sq = v * v
    t = jnp.tanh(v * (KC + (KC * 0.044715) * sq))
    half = 0.5 * (1.0 + t)
    slope = half + (0.5 * v) * (1.0 - t * t) * (KC + (3 * KC * 0.044715) * sq)
    return v * half, slope


def stack_lats(ref, n, v):
    ref[3 * C * n : 3 * C * n + C] = earlier_lat(v).astype(BF16)
    ref[3 * C * n + C : 3 * C * n + 2 * C] = v.astype(BF16)
    ref[3 * C * n + 2 * C : 3 * C * n + 3 * C] = later_lat(v).astype(BF16)


def window(ref, n, rows):
    return jnp.concatenate([ref[rows * n : rows * (n + 3)], ref[rows * (n + 1) : rows * (n + 4)]], axis=1)


def sum_lats(s):
    res = []
    for k in range(2):
        part = s[:, W2 * k : W2 * (k + 1)]
        res.append(earlier_lat(part[:C]) + part[C : 2 * C] + later_lat(part[2 * C :]))
    return res


def step_from(sums, step, total):
    whole = jnp.sum(sums, axis=0, keepdims=True)
    lane = lax.broadcasted_iota(jnp.int32, whole.shape, 1)
    norm = jnp.sum(jnp.where(lane == 0, whole, 0.0), axis=1, keepdims=True)
    return step[:, :1] / jnp.sqrt(norm / total + 1e-06)


def forward_kernel(total, second):
    def kernel(*refs):
        refs = list(refs)
        take = lambda n: [refs.pop(0) for _ in range(n)]
        if second:
            step_ref, sums_ref, g0_ref, ggot0, ggot1 = take(5)
        band_ref, own_ref, got0, got1, o_ref, k2_ref, bias_ref, small_ref = take(8)
        x_ref, m_ref, slope = take(3)
        alpha_ref = take(1)[0] if second else None
        vx, hid = refs
        if second:
            alpha = step_from(sums_ref[...], step_ref[...], total)
            alpha_ref[...] = jnp.broadcast_to(alpha, (1, W2))

        even = (band_ref[...] & 1) == 0

        def at(e, own, zero, one):
            if e < HALO:
                return pick(even, one[e], zero[e])
            if e < HALO + BAND:
                return own[e - HALO]
            return pick(even, zero[e - HALO - BAND], one[e - HALO - BAND])

        for e in range(16):
            v = at(e, own_ref, got0, got1)
            if second:
                v = v - alpha * at(e, g0_ref, ggot0, ggot1)
            if 2 <= e < 14:
                x_ref[e - 2] = v
            stack_lats(vx, e, v)
        bias = bias_ref[...]
        bias2 = jnp.concatenate([bias, bias], axis=1)
        for h in range(0, 14, 2):
            pre = dot(o_ref[...], window(vx, h, 3 * C)) + bias2
            act, sl = gelu_pair(pre)
            for k in range(2):
                n = h + k
                hid[F * n : F * (n + 1)] = act[:, W2 * k : W2 * (k + 1)].astype(BF16)
                if 2 <= n < 12:
                    slope[n - 2] = sl[:, W2 * k : W2 * (k + 1)]
        for o in range(0, 12, 2):
            s = sum_lats(dot(k2_ref[...], window(hid, o, F)))
            for k in range(2):
                m_ref[o + k] = x_ref[o + k] + s[k] + small_ref[0]

    return kernel


def forward(total, ins, second):
    outs = [((12, C, W2), F32), ((12, C, W2), F32), ((10, F, W2), F32)] + ([((1, W2), F32)] if second else [])
    scratch = [pltpu.VMEM((16 * 3 * C, W2), BF16), pltpu.VMEM((14 * F, W2), BF16)]
    return call(forward_kernel(total, second), ins, outs, scratch, limit=16)


def gradient_kernel(second, n_tm, n_all):
    def kernel(*refs):
        refs = list(refs)
        take = lambda n: [refs.pop(0) for _ in range(n)]
        place_ref, band_ref, x_ref, m_ref, slope, got0, got1, r0_ref, s0_ref = take(9)
        if second:
            alpha_ref, ggot0, ggot1, r1_ref, s1_ref = take(5)
        bg_ref, wt_ref, woa_ref, wia_ref, o_ref, k2_ref, bias_ref, small_ref = take(8)
        g_ref, row_ref = take(2)
        send0, send1 = (None, None) if second else take(2)
        vl, hid, ln, gh, vx, hid_prev, x_prev = refs
        place = place_ref[...]
        even_tm = (place & 1) == 0
        even = (band_ref[...] & 1) == 0
        left = lanes() < LAT
        b2, mw, bw = small_ref[0], small_ref[1], small_ref[2]

        def strip(n, ahead):
            one, two = (0, 1) if ahead else (1, 0)
            v = pick(even_tm, (got0, got1)[one][n], (got0, got1)[two][n])
            if second:
                v = v - alpha_ref[...] * pick(even_tm, (ggot0, ggot1)[one][n], (ggot0, ggot1)[two][n])
            return v

        keep = left | (place < n_tm - 1)
        for n in range(6):
            u = strip(n, True)
            for k, part in ((n, halves(u)), (n + 6, u)):
                nxt = jnp.where(left, halves(x_ref[k]), part)
                lv = jnp.where(keep, mw * (nxt - m_ref[k]), 0.0)
                ln[k] = lv
                stack_lats(vl, k, lv)
        dwn = [strip(n, False) for n in range(6)]
        for r in range(8):
            one = dwn[r] if r < 6 else halves(dwn[r - 6])
            two = dwn[r - 2] if r >= 2 else halves(dwn[r + 4])
            v = jnp.where(left, one, two)
            x_prev[r] = v
            stack_lats(vx, r, v)
        bias = bias_ref[...]
        bias2 = jnp.concatenate([bias, bias], axis=1)
        for h in range(0, 6, 2):
            act, _ = gelu_pair(dot(o_ref[...], window(vx, h, 3 * C)) + bias2)
            for k in range(2):
                n = h + k
                hid_prev[F * n : F * (n + 1)] = act[:, W2 * k : W2 * (k + 1)].astype(BF16)
        for h in range(0, 10, 2):
            z = dot(woa_ref[...], window(vl, h, 3 * C))
            for k in range(2):
                n = h + k
                hid[F * n : F * (n + 1)] = (slope[n] * z[:, W2 * k : W2 * (k + 1)]).astype(BF16)
        for o in range(0, BAND, 2):
            s = sum_lats(dot(wia_ref[...], window(hid, o, F)))
            for k in range(2):
                gh[o + k] = ln[o + k + 2] + s[k]
        squares = jnp.zeros((C, W2), F32)
        cost = jnp.zeros((C, W2), F32)
        for o in range(0, 4, 2):
            s = sum_lats(dot(k2_ref[...], window(hid_prev, o, F)))
            for k in range(2):
                m = x_prev[o + k + 2] + s[k] + b2
                sides = []
                for side in range(2):
                    i = o + k + 4 * side
                    x = x_ref[i + 2]
                    before = m if side == 0 else halves(m)
                    first = jnp.where(place > 0, mw * (x - before), 0.0)
                    lo = jnp.where(left, first, halves(ln[i + 2]))
                    dep = jnp.where(left & (place == 0), x - bg_ref[i], 0.0)
                    seen = s0_ref[i]
                    if second:
                        seen = seen - alpha_ref[...] * s1_ref[i]
                    g = lo - gh[i] + seen + bw * dep
                    g_ref[i] = g
                    sides.append(g)
                    squares = squares + g * g
                    cost = cost + lo * lo / mw + bw * dep * dep
                if not second:
                    send0[o + k] = jnp.where(even, sides[1], sides[0]).astype(BF16)
                    send1[o + k] = jnp.where(even, sides[0], sides[1]).astype(BF16)
        r = r0_ref[...]
        if second:
            r = r - alpha_ref[:, :1] * r1_ref[...]
        paid = jnp.sum(wt_ref[...] * r * r, axis=1, keepdims=True)
        norm = jnp.sum(jnp.sum(squares, axis=0, keepdims=True), axis=1, keepdims=True)
        paid = 0.5 * (paid + jnp.sum(jnp.sum(cost, axis=0, keepdims=True), axis=1, keepdims=True))
        lane = lax.broadcasted_iota(jnp.int32, (n_all, W2), 1)
        row_ref[...] = jnp.where(lane == 0, norm, jnp.where(lane == 1, paid, 0.0))

    return kernel


def gradient(n_tm, n_all, ins, second):
    edge = ((HALO, C, W2), BF16)
    outs = [((BAND, C, W2), F32), ((n_all, W2), F32)] + ([] if second else [edge, edge])
    scratch = [pltpu.VMEM((12 * 3 * C, W2), BF16), pltpu.VMEM((10 * F, W2), BF16), pltpu.VMEM((12, C, W2), F32)]
    scratch += [pltpu.VMEM((BAND, C, W2), F32), pltpu.VMEM((8 * 3 * C, W2), BF16), pltpu.VMEM((6 * F, W2), BF16)]
    scratch += [pltpu.VMEM((8, C, W2), F32)]
    return call(gradient_kernel(second, n_tm, n_all), ins, outs, scratch, limit=16)


def final_kernel(total):
    def kernel(step_ref, first_ref, sums_ref, x_ref, g_ref, x_out, cost_out):
        alpha = step_from(sums_ref[...], step_ref[...], total)
        for i in range(BAND):
            v = x_ref[i + 2] - alpha * g_ref[i]
            v = jnp.concatenate([v, jnp.zeros((W2 - C, W2), F32)], axis=0).T[:, :C]
            x_out[0, i] = v[:LAT]
            x_out[1, i] = v[LAT:]
        c0 = jnp.sum(first_ref[...], axis=0, keepdims=True)
        c1 = jnp.sum(sums_ref[...], axis=0, keepdims=True)
        lane = lax.broadcasted_iota(jnp.int32, c0.shape, 1)
        one = jnp.sum(jnp.where(lane == 1, c0, 0.0), axis=1, keepdims=True)
        two = jnp.sum(jnp.where(lane == 1, c1, 0.0), axis=1, keepdims=True)
        cost_out[...] = jnp.where(lane == 0, one, two)[:, :2]

    return kernel


def swapped(value, axes, first):
    n = lax.axis_size(axes)
    closed = axes == LON
    pairs = []
    for i in range(first, n, 2):
        j = (i + 1) % n
        if closed or j > i:
            pairs += [(i, j), (j, i)]
    return lax.ppermute(value, axes, pairs)


def exchange(place, band, mine0, mine1):
    got0 = swapped(mine0, LON, 0)
    got1 = swapped(mine1, LON, 1)
    send0, send1 = strips(place, band, mine0, mine1, got0, got1)
    strip0 = swapped(send0, TM, 0)
    strip1 = swapped(send1, TM, 1)
    return got0, got1, strip0, strip1, send0


def per_device(x, background, opening, b1, closing, b2, mw, bw, cell, chan, val, wt, step):
    n_tm = lax.axis_size(TM)
    n_all = n_tm * lax.axis_size(LON)
    total = float(2 * BAND * C * LAT * n_all)
    place = lax.axis_index(TM).astype(jnp.int32)[None]
    band = lax.axis_index(LON).astype(jnp.int32)[None]
    xp, mine0, mine1, place, band, step, spot, chan, val, wt, b1, small = pack(
        place, band, step[None], jnp.swapaxes(x, 2, 3), (cell, chan, val, wt), (b1, b2, mw, bw)
    )
    got0, got1, strip0, strip1, _ = exchange(place, band, mine0, mine1)
    o, k2, wia, woa, bias, small, bgp = prepare_weights(opening.T, closing, b1, small, jnp.swapaxes(background, 1, 2))
    nets = (o, k2, bias, small)
    own = (band, xp, got0, got1) + nets
    lines = (spot, chan, val, wt)
    x0, m0, slope = forward(total, own, False)
    r0, s0, hot = observe(lines, xp)
    rest = (bgp, wt, woa, wia) + nets
    g0, row, mine0, mine1 = gradient(n_tm, n_all, (place, band, x0, m0, slope, strip0, strip1, r0, s0) + rest, False)
    sums0 = lax.all_to_all(row, TM_LON, 0, 0, tiled=True)
    ggot0, ggot1, gstrip0, gstrip1, sent = exchange(place, band, mine0, mine1)
    later_g0, _ = lax.optimization_barrier((g0, sent))
    x1, m1, slope, alpha = forward(total, (step, sums0, g0, ggot0, ggot1) + own, True)
    r1, s1 = observe(lines, later_g0, hot)
    ins = (place, band, x1, m1, slope, strip0, strip1, r0, s0, alpha, gstrip0, gstrip1, r1, s1)
    g1, row = gradient(n_tm, n_all, ins + rest, True)
    sums1 = lax.all_to_all(row, TM_LON, 0, 0, tiled=True)
    x2, costs = call(
        final_kernel(total),
        [step, sums0, sums1, x1, g1],
        [((2, BAND, LAT, C), F32), ((1, 2), F32)],
    )
    return jnp.swapaxes(x2, 2, 3), costs.reshape(2)


def solution(mesh):
    n_tm, n_lon = mesh.devices.shape
    if (n_tm, n_lon) == (8, 32):
        shape = (4, 2, 2, 8, 2)
    else:
        shape = (n_tm, 1, 1, n_lon // 2, 2)
    split = Mesh(mesh.devices.reshape(shape), TM_LON)
    placed = (
        P(TM, LON, None, None),
        P(LON, None, None),
        P(), P(), P(), P(), P(), P(),
        P(TM, LON), P(TM, LON), P(TM, LON), P(TM, LON),
        P(),
    )
    return jax.shard_map(
        per_device,
        mesh=split,
        in_specs=placed,
        out_specs=(P(TM, LON, None, None), P()),
        check_vma=False,
    )
```

```python
import jax
import jax.numpy as jnp
from jax import lax
from jax.experimental import pallas as pl
from jax.experimental.pallas import tpu as pltpu
from jax.sharding import Mesh
from jax.sharding import PartitionSpec as P


LON = ("lon_0", "lon_1", "lon_2")
TM = ("tm_0", "tm_1")
TM_LON = TM + LON
C = 80
F = 256
LAT = 64
BAND = 8
HALO = 4
OBS = 256
W2 = 2 * LAT
F32 = jnp.float32
BF16 = jnp.bfloat16
KC = 0.7978845608028654


def lanes(rows=C):
    return lax.broadcasted_iota(jnp.int32, (rows, W2), 1)


def call(kernel, ins, outs, scratch=(), limit=8, scalars=0):
    smem = pl.BlockSpec(memory_space=pltpu.SMEM)
    vmem = pl.BlockSpec(memory_space=pltpu.VMEM)
    return pl.pallas_call(
        kernel,
        out_shape=tuple(jax.ShapeDtypeStruct(shape, dtype) for shape, dtype in outs),
        in_specs=[smem] * scalars + [vmem] * (len(ins) - scalars),
        out_specs=tuple(vmem for _ in outs),
        scratch_shapes=list(scratch),
        compiler_params=pltpu.CompilerParams(vmem_limit_bytes=int(limit * 2**20)),
    )(*ins)


def dot(a, b):
    return jnp.dot(a, b, preferred_element_type=F32)


def earlier_lat(v):
    lane = lanes(v.shape[0])
    return jnp.where((lane == 0) | (lane == LAT), 0.0, pltpu.roll(v, 1, 1))


def later_lat(v):
    lane = lanes(v.shape[0])
    return jnp.where((lane == LAT - 1) | (lane == W2 - 1), 0.0, pltpu.roll(v, W2 - 1, 1))


def halves(v):
    return pltpu.roll(v, LAT, 1)


def pick(even, one, two):
    return jnp.where(even, one.astype(F32), two.astype(F32))


def pack_kernel(place_ref, band_ref, step_ref, x_ref, xp_ref, s0_ref, s1_ref, place_row, band_row, step_row):
    place_row[...] = jnp.full((1, W2), place_ref[0], jnp.int32)
    band_row[...] = jnp.full((1, W2), band_ref[0], jnp.int32)
    step_row[...] = jnp.full((1, W2), step_ref[0], F32)
    even = (jnp.full((1, W2), band_ref[0], jnp.int32) & 1) == 0
    for i in range(HALO):
        one = jnp.concatenate([x_ref[0, i], x_ref[1, i]], axis=0).T
        two = jnp.concatenate([x_ref[0, i + HALO], x_ref[1, i + HALO]], axis=0).T
        xp_ref[i] = one
        xp_ref[i + HALO] = two
        s0_ref[i] = jnp.where(even, two, one).astype(BF16)
        s1_ref[i] = jnp.where(even, one, two).astype(BF16)


def pack(place, band, step, x):
    edge = ((HALO, C, W2), BF16)
    row = lambda n, dtype: ((1, n), dtype)
    outs = [((BAND, C, W2), F32), edge, edge, row(W2, jnp.int32), row(W2, jnp.int32), row(W2, F32)]
    return call(pack_kernel, [place, band, step, x], outs, limit=8, scalars=3)


def weights_kernel(ot_ref, c_ref, b1_ref, b2_ref, mw_ref, bw_ref, bg_ref,
                   o_ref, k2_ref, wia_ref, woa_ref, bias_ref, small_ref, bgp_ref, tall, row):
    tall[9 * C :, :] = jnp.zeros((768 - 9 * C, F), F32)
    tall[: 9 * C, :] = ot_ref[...].astype(F32)
    o_ref[...] = tall[...].T[:, : 9 * C].astype(BF16)
    turned = ot_ref
    for t in range(9):
        a, b = divmod(t, 3)
        block = c_ref[:, F * t : F * (t + 1)]
        k2_ref[C * b : C * (b + 1), F * a : F * (a + 1)] = block
        tall[C * (8 - t) : C * (9 - t), :] = block.astype(F32)
        wia_ref[C * b : C * (b + 1), F * a : F * (a + 1)] = turned[C * (8 - t) : C * (9 - t), :]
    back = tall[...].T
    woa_ref[...] = back[:, : 9 * C].astype(BF16)
    bias_ref[...] = jnp.broadcast_to(b1_ref[...], (W2, F)).T
    row[...] = jnp.zeros((W2, W2), F32)
    for n, ref in enumerate((b2_ref, mw_ref, bw_ref)):
        row[:, :C] = jnp.broadcast_to(ref[...], (W2, C))
        small_ref[n] = row[...].T[:C]
    for i in range(BAND):
        bgp_ref[i] = jnp.concatenate([bg_ref[i], jnp.zeros((LAT, C), F32)], axis=0).T


def prepare_weights(opening_t, closing, b1, b2, mw, bw, bg):
    ins = [opening_t, closing, b1[None], b2[None], mw[None], bw[None], bg]
    outs = [((F, 9 * C), BF16), ((3 * C, 3 * F), BF16), ((3 * C, 3 * F), BF16), ((F, 9 * C), BF16)]
    outs += [((F, W2), F32), ((3, C, W2), F32), ((BAND, C, W2), F32)]
    return call(
        weights_kernel,
        ins,
        outs,
        [pltpu.VMEM((768, F), F32), pltpu.VMEM((W2, W2), F32)],
        limit=8,
    )


def split3(v):
    hi = v.astype(BF16)
    rest = v - hi.astype(F32)
    mid = rest.astype(BF16)
    low = (rest - mid.astype(F32)).astype(BF16)
    return jnp.concatenate([hi, mid, low], axis=0)


def join3(v):
    return (v[2 * C :] + v[C : 2 * C]) + v[:C]


def lines(ref):
    return jnp.concatenate([ref[0:1, :], ref[1:2, :]], axis=1)


def first_obs_kernel(cell_ref, chan_ref, val_ref, wt_ref, x_ref, r_ref, s_ref, hot, chan_row, wt_row):
    cell = lines(cell_ref)
    sub = (lax.broadcasted_iota(jnp.int32, cell.shape, 1) >= OBS).astype(jnp.int32)
    spot = (cell >> 6) * W2 + sub * LAT + (cell & (LAT - 1))
    rows = 2 * W2
    for p in range(BAND // 2):
        at = lax.broadcasted_iota(jnp.int32, (rows, 2 * OBS), 0) + p * rows
        hot[p] = jnp.where(at == spot, 1.0, 0.0).astype(BF16)
    chan_row[...] = lines(chan_ref)
    wt_row[...] = lines(wt_ref)
    watch(chan_row, wt_row, hot, x_ref, r_ref, s_ref, lines(val_ref))


def later_obs_kernel(chan_row, wt_row, hot, x_ref, r_ref, s_ref):
    watch(chan_row, wt_row, hot, x_ref, r_ref, s_ref, None)


def watch(chan_ref, wt_ref, hot, x_ref, r_ref, s_ref, val):
    total = jnp.zeros((3 * C, 2 * OBS), F32)
    for p in range(BAND // 2):
        total = total + dot(split3(jnp.concatenate([x_ref[2 * p], x_ref[2 * p + 1]], axis=1)), hot[p])
    mine = lax.broadcasted_iota(jnp.int32, (C, 2 * OBS), 0) == chan_ref[...]
    r = jnp.sum(jnp.where(mine, join3(total), 0.0), axis=0, keepdims=True)
    if val is not None:
        r = r - val
    r_ref[...] = r
    spread = split3(jnp.where(mine, wt_ref[...] * r, 0.0))
    for p in range(BAND // 2):
        got = lax.dot_general(spread, hot[p], (((1,), (1,)), ((), ())), preferred_element_type=F32)
        got = join3(got)
        s_ref[2 * p] = got[:, :W2]
        s_ref[2 * p + 1] = got[:, W2:]


SEEN = [((1, 2 * OBS), F32), ((BAND, C, W2), F32)]


def observe_first(cell, chan, val, wt, field):
    more = [((BAND // 2, 2 * W2, 2 * OBS), BF16), ((1, 2 * OBS), jnp.int32), ((1, 2 * OBS), F32)]
    return call(first_obs_kernel, [cell, chan, val, wt, field], SEEN + more, limit=8)


def observe_later(chan, wt, hot, field):
    return call(later_obs_kernel, [chan, wt, hot, field], SEEN, limit=8)


def strip_kernel(place_ref, band_ref, mine0, mine1, got0, got1, send0, send1):
    even = (band_ref[...] & 1) == 0
    even_tm = (place_ref[...] & 1) == 0

    def at(e):
        if e < 0:
            return pick(even, got1[HALO + e], got0[HALO + e])
        if e < HALO:
            return pick(even, mine1[e], mine0[e])
        if e < BAND:
            return pick(even, mine0[e - HALO], mine1[e - HALO])
        return pick(even, got0[e - BAND], got1[e - BAND])

    left = lanes() < LAT
    for p in range(6):
        one, two = at(p - 2), at(p + 4)
        up = jnp.where(left, one, halves(two))
        down = jnp.where(left, halves(one), two)
        send0[p] = jnp.where(even_tm, down, up).astype(BF16)
        send1[p] = jnp.where(even_tm, up, down).astype(BF16)


def strips(*args):
    strip = ((6, C, W2), BF16)
    return call(strip_kernel, list(args), [strip, strip])


def gelu_pair(v):
    sq = v * v
    t = jnp.tanh(v * (KC + (KC * 0.044715) * sq))
    half = 0.5 * (1.0 + t)
    slope = half + (0.5 * v) * (1.0 - t * t) * (KC + (3 * KC * 0.044715) * sq)
    return v * half, slope


def stack_lats(ref, n, v):
    ref[3 * C * n : 3 * C * n + C] = earlier_lat(v).astype(BF16)
    ref[3 * C * n + C : 3 * C * n + 2 * C] = v.astype(BF16)
    ref[3 * C * n + 2 * C : 3 * C * n + 3 * C] = later_lat(v).astype(BF16)


def window(ref, n, rows):
    return jnp.concatenate([ref[rows * n : rows * (n + 3)], ref[rows * (n + 1) : rows * (n + 4)]], axis=1)


def sum_lats(s):
    res = []
    for k in range(2):
        part = s[:, W2 * k : W2 * (k + 1)]
        res.append(earlier_lat(part[:C]) + part[C : 2 * C] + later_lat(part[2 * C :]))
    return res


def step_from(sums, step, total):
    whole = jnp.sum(sums, axis=0, keepdims=True)
    lane = lax.broadcasted_iota(jnp.int32, whole.shape, 1)
    norm = jnp.sum(jnp.where(lane == 0, whole, 0.0), axis=1, keepdims=True)
    return step[:, :1] / jnp.sqrt(norm / total + 1e-06)


def forward_kernel(total, second):
    def kernel(*refs):
        refs = list(refs)
        take = lambda n: [refs.pop(0) for _ in range(n)]
        if second:
            step_ref, sums_ref, g0_ref, ggot0, ggot1 = take(5)
        band_ref, own_ref, got0, got1, o_ref, k2_ref, bias_ref, small_ref = take(8)
        x_ref, m_ref, slope = take(3)
        alpha_ref = take(1)[0] if second else None
        vx, hid = refs
        if second:
            alpha = step_from(sums_ref[...], step_ref[...], total)
            alpha_ref[...] = jnp.broadcast_to(alpha, (1, W2))

        even = (band_ref[...] & 1) == 0

        def at(e, own, zero, one):
            if e < HALO:
                return pick(even, one[e], zero[e])
            if e < HALO + BAND:
                return own[e - HALO]
            return pick(even, zero[e - HALO - BAND], one[e - HALO - BAND])

        for e in range(16):
            v = at(e, own_ref, got0, got1)
            if second:
                v = v - alpha * at(e, g0_ref, ggot0, ggot1)
            if 2 <= e < 14:
                x_ref[e - 2] = v
            stack_lats(vx, e, v)
        bias = bias_ref[...]
        bias2 = jnp.concatenate([bias, bias], axis=1)
        for h in range(0, 14, 2):
            pre = dot(o_ref[...], window(vx, h, 3 * C)) + bias2
            act, sl = gelu_pair(pre)
            for k in range(2):
                n = h + k
                hid[F * n : F * (n + 1)] = act[:, W2 * k : W2 * (k + 1)].astype(BF16)
                if 2 <= n < 12:
                    slope[n - 2] = sl[:, W2 * k : W2 * (k + 1)]
        for o in range(0, 12, 2):
            s = sum_lats(dot(k2_ref[...], window(hid, o, F)))
            for k in range(2):
                m_ref[o + k] = x_ref[o + k] + s[k] + small_ref[0]

    return kernel


def forward(total, ins, second):
    outs = [((12, C, W2), F32), ((12, C, W2), F32), ((10, F, W2), F32)] + ([((1, W2), F32)] if second else [])
    scratch = [pltpu.VMEM((16 * 3 * C, W2), BF16), pltpu.VMEM((14 * F, W2), BF16)]
    return call(forward_kernel(total, second), ins, outs, scratch, limit=16)


def gradient_kernel(second, n_tm, n_all):
    def kernel(*refs):
        refs = list(refs)
        take = lambda n: [refs.pop(0) for _ in range(n)]
        place_ref, band_ref, x_ref, m_ref, slope, got0, got1, r0_ref, s0_ref = take(9)
        if second:
            alpha_ref, ggot0, ggot1, r1_ref, s1_ref = take(5)
        bg_ref, wt_ref, woa_ref, wia_ref, o_ref, k2_ref, bias_ref, small_ref = take(8)
        g_ref, row_ref = take(2)
        send0, send1 = (None, None) if second else take(2)
        vl, hid, ln, gh, vx, hid_prev, x_prev = refs
        place = place_ref[...]
        even_tm = (place & 1) == 0
        even = (band_ref[...] & 1) == 0
        left = lanes() < LAT
        b2, mw, bw = small_ref[0], small_ref[1], small_ref[2]

        def strip(n, ahead):
            one, two = (0, 1) if ahead else (1, 0)
            v = pick(even_tm, (got0, got1)[one][n], (got0, got1)[two][n])
            if second:
                v = v - alpha_ref[...] * pick(even_tm, (ggot0, ggot1)[one][n], (ggot0, ggot1)[two][n])
            return v

        keep = left | (place < n_tm - 1)
        for n in range(6):
            u = strip(n, True)
            for k, part in ((n, halves(u)), (n + 6, u)):
                nxt = jnp.where(left, halves(x_ref[k]), part)
                lv = jnp.where(keep, mw * (nxt - m_ref[k]), 0.0)
                ln[k] = lv
                stack_lats(vl, k, lv)
        dwn = [strip(n, False) for n in range(6)]
        for r in range(8):
            one = dwn[r] if r < 6 else halves(dwn[r - 6])
            two = dwn[r - 2] if r >= 2 else halves(dwn[r + 4])
            v = jnp.where(left, one, two)
            x_prev[r] = v
            stack_lats(vx, r, v)
        bias = bias_ref[...]
        bias2 = jnp.concatenate([bias, bias], axis=1)
        for h in range(0, 6, 2):
            act, _ = gelu_pair(dot(o_ref[...], window(vx, h, 3 * C)) + bias2)
            for k in range(2):
                n = h + k
                hid_prev[F * n : F * (n + 1)] = act[:, W2 * k : W2 * (k + 1)].astype(BF16)
        for h in range(0, 10, 2):
            z = dot(woa_ref[...], window(vl, h, 3 * C))
            for k in range(2):
                n = h + k
                hid[F * n : F * (n + 1)] = (slope[n] * z[:, W2 * k : W2 * (k + 1)]).astype(BF16)
        for o in range(0, BAND, 2):
            s = sum_lats(dot(wia_ref[...], window(hid, o, F)))
            for k in range(2):
                gh[o + k] = ln[o + k + 2] + s[k]
        squares = jnp.zeros((C, W2), F32)
        cost = jnp.zeros((C, W2), F32)
        for o in range(0, 4, 2):
            s = sum_lats(dot(k2_ref[...], window(hid_prev, o, F)))
            for k in range(2):
                m = x_prev[o + k + 2] + s[k] + b2
                sides = []
                for side in range(2):
                    i = o + k + 4 * side
                    x = x_ref[i + 2]
                    before = m if side == 0 else halves(m)
                    first = jnp.where(place > 0, mw * (x - before), 0.0)
                    lo = jnp.where(left, first, halves(ln[i + 2]))
                    dep = jnp.where(left & (place == 0), x - bg_ref[i], 0.0)
                    seen = s0_ref[i]
                    if second:
                        seen = seen - alpha_ref[...] * s1_ref[i]
                    g = lo - gh[i] + seen + bw * dep
                    g_ref[i] = g
                    sides.append(g)
                    squares = squares + g * g
                    cost = cost + lo * lo / mw + bw * dep * dep
                if not second:
                    send0[o + k] = jnp.where(even, sides[1], sides[0]).astype(BF16)
                    send1[o + k] = jnp.where(even, sides[0], sides[1]).astype(BF16)
        r = r0_ref[...]
        if second:
            r = r - alpha_ref[:, :1] * r1_ref[...]
        paid = jnp.sum(wt_ref[...] * r * r, axis=1, keepdims=True)
        norm = jnp.sum(jnp.sum(squares, axis=0, keepdims=True), axis=1, keepdims=True)
        paid = 0.5 * (paid + jnp.sum(jnp.sum(cost, axis=0, keepdims=True), axis=1, keepdims=True))
        lane = lax.broadcasted_iota(jnp.int32, (n_all, W2), 1)
        row_ref[...] = jnp.where(lane == 0, norm, jnp.where(lane == 1, paid, 0.0))

    return kernel


def gradient(n_tm, n_all, ins, second):
    edge = ((HALO, C, W2), BF16)
    outs = [((BAND, C, W2), F32), ((n_all, W2), F32)] + ([] if second else [edge, edge])
    scratch = [pltpu.VMEM((12 * 3 * C, W2), BF16), pltpu.VMEM((10 * F, W2), BF16), pltpu.VMEM((12, C, W2), F32)]
    scratch += [pltpu.VMEM((BAND, C, W2), F32), pltpu.VMEM((8 * 3 * C, W2), BF16), pltpu.VMEM((6 * F, W2), BF16)]
    scratch += [pltpu.VMEM((8, C, W2), F32)]
    return call(gradient_kernel(second, n_tm, n_all), ins, outs, scratch, limit=16)


def final_kernel(total):
    def kernel(step_ref, first_ref, sums_ref, x_ref, g_ref, x_out, cost_out):
        alpha = step_from(sums_ref[...], step_ref[...], total)
        for i in range(BAND):
            v = x_ref[i + 2] - alpha * g_ref[i]
            v = jnp.concatenate([v, jnp.zeros((W2 - C, W2), F32)], axis=0).T[:, :C]
            x_out[0, i] = v[:LAT]
            x_out[1, i] = v[LAT:]
        c0 = jnp.sum(first_ref[...], axis=0, keepdims=True)
        c1 = jnp.sum(sums_ref[...], axis=0, keepdims=True)
        lane = lax.broadcasted_iota(jnp.int32, c0.shape, 1)
        one = jnp.sum(jnp.where(lane == 1, c0, 0.0), axis=1, keepdims=True)
        two = jnp.sum(jnp.where(lane == 1, c1, 0.0), axis=1, keepdims=True)
        cost_out[...] = jnp.where(lane == 0, one, two)[:, :2]

    return kernel


def swapped(value, axes, first):
    n = lax.axis_size(axes)
    closed = axes == LON
    pairs = []
    for i in range(first, n, 2):
        j = (i + 1) % n
        if closed or j > i:
            pairs += [(i, j), (j, i)]
    return lax.ppermute(value, axes, pairs)


def exchange(place, band, mine0, mine1):
    got0 = swapped(mine0, LON, 0)
    got1 = swapped(mine1, LON, 1)
    send0, send1 = strips(place, band, mine0, mine1, got0, got1)
    strip0 = swapped(send0, TM, 0)
    strip1 = swapped(send1, TM, 1)
    return got0, got1, strip0, strip1, send0


def per_device(x, background, opening, b1, closing, b2, mw, bw, cell, chan, val, wt, step):
    n_tm = lax.axis_size(TM)
    n_all = n_tm * lax.axis_size(LON)
    total = float(2 * BAND * C * LAT * n_all)
    place = lax.axis_index(TM).astype(jnp.int32)[None]
    band = lax.axis_index(LON).astype(jnp.int32)[None]
    xp, mine0, mine1, place, band, step = pack(place, band, step[None], jnp.swapaxes(x, 2, 3))
    got0, got1, strip0, strip1, _ = exchange(place, band, mine0, mine1)
    o, k2, wia, woa, bias, small, bgp = prepare_weights(
        opening.T, closing, b1, b2, mw, bw, jnp.swapaxes(background, 1, 2)
    )
    nets = (o, k2, bias, small)
    own = (band, xp, got0, got1) + nets
    x0, m0, slope = forward(total, own, False)
    r0, s0, hot, chan, wt = observe_first(cell, chan, val, wt, xp)
    rest = (bgp, wt, woa, wia) + nets
    g0, row, mine0, mine1 = gradient(n_tm, n_all, (place, band, x0, m0, slope, strip0, strip1, r0, s0) + rest, False)
    sums0 = lax.all_to_all(row, TM_LON, 0, 0, tiled=True)
    ggot0, ggot1, gstrip0, gstrip1, sent = exchange(place, band, mine0, mine1)
    later_g0, _ = lax.optimization_barrier((g0, sent))
    x1, m1, slope, alpha = forward(total, (step, sums0, g0, ggot0, ggot1) + own, True)
    r1, s1 = observe_later(chan, wt, hot, later_g0)
    ins = (place, band, x1, m1, slope, strip0, strip1, r0, s0, alpha, gstrip0, gstrip1, r1, s1)
    g1, row = gradient(n_tm, n_all, ins + rest, True)
    sums1 = lax.all_to_all(row, TM_LON, 0, 0, tiled=True)
    x2, costs = call(
        final_kernel(total),
        [step, sums0, sums1, x1, g1],
        [((2, BAND, LAT, C), F32), ((1, 2), F32)],
    )
    return jnp.swapaxes(x2, 2, 3), costs.reshape(2)


def solution(mesh):
    n_tm, n_lon = mesh.devices.shape
    if (n_tm, n_lon) == (8, 32):
        shape = (4, 2, 2, 8, 2)
    else:
        shape = (n_tm, 1, 1, n_lon // 2, 2)
    split = Mesh(mesh.devices.reshape(shape), TM_LON)
    placed = (
        P(TM, LON, None, None),
        P(LON, None, None),
        P(), P(), P(), P(), P(), P(),
        P(TM, LON), P(TM, LON), P(TM, LON), P(TM, LON),
        P(),
    )
    return jax.shard_map(
        per_device,
        mesh=split,
        in_specs=placed,
        out_specs=(P(TM, LON, None, None), P()),
        check_vma=False,
    )
```

```python
import jax
import jax.numpy as jnp
from jax import lax
from jax.experimental import pallas as pl
from jax.experimental.pallas import tpu as pltpu
from jax.sharding import Mesh
from jax.sharding import PartitionSpec as P


LON = ("lon_0", "lon_1", "lon_2")
TM = ("tm_0", "tm_1")
TM_LON = TM + LON
C = 80
F = 256
LAT = 64
BAND = 8
HALO = 4
OBS = 256
W2 = 2 * LAT
F32 = jnp.float32
BF16 = jnp.bfloat16
KC = 0.7978845608028654


def lanes(rows=C):
    return lax.broadcasted_iota(jnp.int32, (rows, W2), 1)


def call(kernel, ins, outs, scratch=(), limit=8, scalars=0, far=0):
    smem = pl.BlockSpec(memory_space=pltpu.SMEM)
    vmem = pl.BlockSpec(memory_space=pltpu.VMEM)
    return pl.pallas_call(
        kernel,
        out_shape=tuple(jax.ShapeDtypeStruct(shape, dtype) for shape, dtype in outs),
        in_specs=[smem] * scalars + [vmem] * (len(ins) - scalars),
        out_specs=tuple(pl.BlockSpec(memory_space=pl.ANY) if n < far else vmem for n in range(len(outs))),
        scratch_shapes=list(scratch),
        compiler_params=pltpu.CompilerParams(vmem_limit_bytes=int(limit * 2**20)),
    )(*ins)


def dot(a, b):
    return jnp.dot(a, b, preferred_element_type=F32)


def earlier_lat(v):
    lane = lanes(v.shape[0])
    return jnp.where((lane == 0) | (lane == LAT), 0.0, pltpu.roll(v, 1, 1))


def later_lat(v):
    lane = lanes(v.shape[0])
    return jnp.where((lane == LAT - 1) | (lane == W2 - 1), 0.0, pltpu.roll(v, W2 - 1, 1))


def halves(v):
    return pltpu.roll(v, LAT, 1)


def pick(even, one, two):
    return jnp.where(even, one.astype(F32), two.astype(F32))


def pack_kernel(place_ref, band_ref, step_ref, x_ref, xp_ref, s0_ref, s1_ref, place_row, band_row, step_row):
    place_row[...] = jnp.full((1, W2), place_ref[0], jnp.int32)
    band_row[...] = jnp.full((1, W2), band_ref[0], jnp.int32)
    step_row[...] = jnp.full((1, W2), step_ref[0], F32)
    even = (jnp.full((1, W2), band_ref[0], jnp.int32) & 1) == 0
    for i in range(HALO):
        one = jnp.concatenate([x_ref[0, i], x_ref[1, i]], axis=0).T
        two = jnp.concatenate([x_ref[0, i + HALO], x_ref[1, i + HALO]], axis=0).T
        xp_ref[i] = one
        xp_ref[i + HALO] = two
        s0_ref[i] = jnp.where(even, two, one).astype(BF16)
        s1_ref[i] = jnp.where(even, one, two).astype(BF16)


def pack(place, band, step, x):
    edge = ((HALO, C, W2), BF16)
    row = lambda n, dtype: ((1, n), dtype)
    outs = [((BAND, C, W2), F32), edge, edge, row(W2, jnp.int32), row(W2, jnp.int32), row(W2, F32)]
    return call(pack_kernel, [place, band, step, x], outs, limit=8, scalars=3)


def weights_kernel(ot_ref, c_ref, b1_ref, b2_ref, mw_ref, bw_ref, bg_ref,
                   o_ref, k2_ref, wia_ref, woa_ref, bias_ref, small_ref, bgp_ref, tall, row):
    tall[9 * C :, :] = jnp.zeros((768 - 9 * C, F), F32)
    tall[: 9 * C, :] = ot_ref[...].astype(F32)
    o_ref[...] = tall[...].T[:, : 9 * C].astype(BF16)
    turned = ot_ref
    for t in range(9):
        a, b = divmod(t, 3)
        block = c_ref[:, F * t : F * (t + 1)]
        k2_ref[C * b : C * (b + 1), F * a : F * (a + 1)] = block
        tall[C * (8 - t) : C * (9 - t), :] = block.astype(F32)
        wia_ref[C * b : C * (b + 1), F * a : F * (a + 1)] = turned[C * (8 - t) : C * (9 - t), :]
    back = tall[...].T
    woa_ref[...] = back[:, : 9 * C].astype(BF16)
    bias_ref[...] = jnp.broadcast_to(b1_ref[...], (W2, F)).T
    row[...] = jnp.zeros((W2, W2), F32)
    for n, ref in enumerate((b2_ref, mw_ref, bw_ref)):
        row[:, :C] = jnp.broadcast_to(ref[...], (W2, C))
        small_ref[n] = row[...].T[:C]
    for i in range(BAND):
        bgp_ref[i] = jnp.concatenate([bg_ref[i], jnp.zeros((LAT, C), F32)], axis=0).T


def prepare_weights(opening_t, closing, b1, b2, mw, bw, bg):
    ins = [opening_t, closing, b1[None], b2[None], mw[None], bw[None], bg]
    outs = [((F, 9 * C), BF16), ((3 * C, 3 * F), BF16), ((3 * C, 3 * F), BF16), ((F, 9 * C), BF16)]
    outs += [((F, W2), F32), ((3, C, W2), F32), ((BAND, C, W2), F32)]
    return call(
        weights_kernel,
        ins,
        outs,
        [pltpu.VMEM((768, F), F32), pltpu.VMEM((W2, W2), F32)],
        limit=8,
    )


def split3(v):
    hi = v.astype(BF16)
    rest = v - hi.astype(F32)
    mid = rest.astype(BF16)
    low = (rest - mid.astype(F32)).astype(BF16)
    return jnp.concatenate([hi, mid, low], axis=0)


def join3(v):
    return (v[2 * C :] + v[C : 2 * C]) + v[:C]


def lines(ref):
    return jnp.concatenate([ref[0:1, :], ref[1:2, :]], axis=1)


def first_obs_kernel(cell_ref, chan_ref, val_ref, wt_ref, x_ref, r_ref, s_ref, hot, chan_row, wt_row):
    cell = lines(cell_ref)
    sub = (lax.broadcasted_iota(jnp.int32, cell.shape, 1) >= OBS).astype(jnp.int32)
    spot = (cell >> 6) * W2 + sub * LAT + (cell & (LAT - 1))
    rows = 2 * W2
    for p in range(BAND // 2):
        at = lax.broadcasted_iota(jnp.int32, (rows, 2 * OBS), 0) + p * rows
        hot[p] = jnp.where(at == spot, 1.0, 0.0).astype(BF16)
    chan_row[...] = lines(chan_ref)
    wt_row[...] = lines(wt_ref)
    watch(chan_row, wt_row, hot, x_ref, r_ref, s_ref, lines(val_ref))


def later_obs_kernel(chan_row, wt_row, hot, x_ref, r_ref, s_ref):
    watch(chan_row, wt_row, hot, x_ref, r_ref, s_ref, None)


def watch(chan_ref, wt_ref, hot, x_ref, r_ref, s_ref, val):
    total = jnp.zeros((3 * C, 2 * OBS), F32)
    for p in range(BAND // 2):
        total = total + dot(split3(jnp.concatenate([x_ref[2 * p], x_ref[2 * p + 1]], axis=1)), hot[p])
    mine = lax.broadcasted_iota(jnp.int32, (C, 2 * OBS), 0) == chan_ref[...]
    r = jnp.sum(jnp.where(mine, join3(total), 0.0), axis=0, keepdims=True)
    if val is not None:
        r = r - val
    r_ref[...] = r
    spread = split3(jnp.where(mine, wt_ref[...] * r, 0.0))
    for p in range(BAND // 2):
        got = lax.dot_general(spread, hot[p], (((1,), (1,)), ((), ())), preferred_element_type=F32)
        got = join3(got)
        s_ref[2 * p] = got[:, :W2]
        s_ref[2 * p + 1] = got[:, W2:]


SEEN = [((1, 2 * OBS), F32), ((BAND, C, W2), F32)]


def observe_first(cell, chan, val, wt, field):
    more = [((BAND // 2, 2 * W2, 2 * OBS), BF16), ((1, 2 * OBS), jnp.int32), ((1, 2 * OBS), F32)]
    return call(first_obs_kernel, [cell, chan, val, wt, field], SEEN + more, limit=8)


def observe_later(chan, wt, hot, field):
    return call(later_obs_kernel, [chan, wt, hot, field], SEEN, limit=8)


def strip_kernel(place_ref, band_ref, mine0, mine1, got0, got1, send0, send1):
    even = (band_ref[...] & 1) == 0
    even_tm = (place_ref[...] & 1) == 0

    def at(e):
        if e < 0:
            return pick(even, got1[HALO + e], got0[HALO + e])
        if e < HALO:
            return pick(even, mine1[e], mine0[e])
        if e < BAND:
            return pick(even, mine0[e - HALO], mine1[e - HALO])
        return pick(even, got0[e - BAND], got1[e - BAND])

    left = lanes() < LAT
    for p in range(6):
        one, two = at(p - 2), at(p + 4)
        up = jnp.where(left, one, halves(two))
        down = jnp.where(left, halves(one), two)
        send0[p] = jnp.where(even_tm, down, up).astype(BF16)
        send1[p] = jnp.where(even_tm, up, down).astype(BF16)


def strips(*args):
    strip = ((6, C, W2), BF16)
    return call(strip_kernel, list(args), [strip, strip])


def gelu_pair(v):
    sq = v * v
    t = jnp.tanh(v * (KC + (KC * 0.044715) * sq))
    half = 0.5 * (1.0 + t)
    slope = half + (0.5 * v) * (1.0 - t * t) * (KC + (3 * KC * 0.044715) * sq)
    return v * half, slope


def stack_lats(ref, n, v):
    ref[3 * C * n : 3 * C * n + C] = earlier_lat(v).astype(BF16)
    ref[3 * C * n + C : 3 * C * n + 2 * C] = v.astype(BF16)
    ref[3 * C * n + 2 * C : 3 * C * n + 3 * C] = later_lat(v).astype(BF16)


def window(ref, n, rows):
    return jnp.concatenate([ref[rows * n : rows * (n + 3)], ref[rows * (n + 1) : rows * (n + 4)]], axis=1)


def sum_lats(s):
    res = []
    for k in range(2):
        part = s[:, W2 * k : W2 * (k + 1)]
        res.append(earlier_lat(part[:C]) + part[C : 2 * C] + later_lat(part[2 * C :]))
    return res


def step_from(sums, step, total):
    whole = jnp.sum(sums, axis=0, keepdims=True)
    lane = lax.broadcasted_iota(jnp.int32, whole.shape, 1)
    norm = jnp.sum(jnp.where(lane == 0, whole, 0.0), axis=1, keepdims=True)
    return step[:, :1] / jnp.sqrt(norm / total + 1e-06)


def forward_kernel(total, second):
    def kernel(*refs):
        refs = list(refs)
        take = lambda n: [refs.pop(0) for _ in range(n)]
        if second:
            step_ref, sums_ref, g0_ref, ggot0, ggot1 = take(5)
        band_ref, own_ref, got0, got1, o_ref, k2_ref, bias_ref, small_ref = take(8)
        x_ref, m_ref, slope = take(3)
        alpha_ref = take(1)[0] if second else None
        vx, hid = refs
        if second:
            alpha = step_from(sums_ref[...], step_ref[...], total)
            alpha_ref[...] = jnp.broadcast_to(alpha, (1, W2))

        even = (band_ref[...] & 1) == 0

        def at(e, own, zero, one):
            if e < HALO:
                return pick(even, one[e], zero[e])
            if e < HALO + BAND:
                return own[e - HALO]
            return pick(even, zero[e - HALO - BAND], one[e - HALO - BAND])

        for e in range(16):
            v = at(e, own_ref, got0, got1)
            if second:
                v = v - alpha * at(e, g0_ref, ggot0, ggot1)
            if 2 <= e < 14:
                x_ref[e - 2] = v
            stack_lats(vx, e, v)
        bias = bias_ref[...]
        bias2 = jnp.concatenate([bias, bias], axis=1)
        for h in range(0, 14, 2):
            pre = dot(o_ref[...], window(vx, h, 3 * C)) + bias2
            act, sl = gelu_pair(pre)
            for k in range(2):
                n = h + k
                hid[F * n : F * (n + 1)] = act[:, W2 * k : W2 * (k + 1)].astype(BF16)
                if 2 <= n < 12:
                    slope[n - 2] = sl[:, W2 * k : W2 * (k + 1)]
        for o in range(0, 12, 2):
            s = sum_lats(dot(k2_ref[...], window(hid, o, F)))
            for k in range(2):
                m_ref[o + k] = x_ref[o + k] + s[k] + small_ref[0]

    return kernel


def forward(total, ins, second):
    outs = [((12, C, W2), F32), ((12, C, W2), F32), ((10, F, W2), F32)] + ([((1, W2), F32)] if second else [])
    scratch = [pltpu.VMEM((16 * 3 * C, W2), BF16), pltpu.VMEM((14 * F, W2), BF16)]
    return call(forward_kernel(total, second), ins, outs, scratch, limit=16)


def gradient_kernel(second, n_tm, n_all):
    def kernel(*refs):
        refs = list(refs)
        take = lambda n: [refs.pop(0) for _ in range(n)]
        place_ref, band_ref, x_ref, m_ref, slope, got0, got1, r0_ref, s0_ref = take(9)
        if second:
            alpha_ref, ggot0, ggot1, r1_ref, s1_ref = take(5)
        bg_ref, wt_ref, woa_ref, wia_ref, o_ref, k2_ref, bias_ref, small_ref = take(8)
        g_ref, row_ref = take(2)
        send0, send1 = (None, None) if second else take(2)
        vl, hid, ln, gh, vx, hid_prev, x_prev = refs
        place = place_ref[...]
        even_tm = (place & 1) == 0
        even = (band_ref[...] & 1) == 0
        left = lanes() < LAT
        b2, mw, bw = small_ref[0], small_ref[1], small_ref[2]

        def strip(n, ahead):
            one, two = (0, 1) if ahead else (1, 0)
            v = pick(even_tm, (got0, got1)[one][n], (got0, got1)[two][n])
            if second:
                v = v - alpha_ref[...] * pick(even_tm, (ggot0, ggot1)[one][n], (ggot0, ggot1)[two][n])
            return v

        keep = left | (place < n_tm - 1)
        for n in range(6):
            u = strip(n, True)
            for k, part in ((n, halves(u)), (n + 6, u)):
                nxt = jnp.where(left, halves(x_ref[k]), part)
                lv = jnp.where(keep, mw * (nxt - m_ref[k]), 0.0)
                ln[k] = lv
                stack_lats(vl, k, lv)
        dwn = [strip(n, False) for n in range(6)]
        for r in range(8):
            one = dwn[r] if r < 6 else halves(dwn[r - 6])
            two = dwn[r - 2] if r >= 2 else halves(dwn[r + 4])
            v = jnp.where(left, one, two)
            x_prev[r] = v
            stack_lats(vx, r, v)
        bias = bias_ref[...]
        bias2 = jnp.concatenate([bias, bias], axis=1)
        for h in range(0, 6, 2):
            act, _ = gelu_pair(dot(o_ref[...], window(vx, h, 3 * C)) + bias2)
            for k in range(2):
                n = h + k
                hid_prev[F * n : F * (n + 1)] = act[:, W2 * k : W2 * (k + 1)].astype(BF16)
        for h in range(0, 10, 2):
            z = dot(woa_ref[...], window(vl, h, 3 * C))
            for k in range(2):
                n = h + k
                hid[F * n : F * (n + 1)] = (slope[n] * z[:, W2 * k : W2 * (k + 1)]).astype(BF16)
        for o in range(0, BAND, 2):
            s = sum_lats(dot(wia_ref[...], window(hid, o, F)))
            for k in range(2):
                gh[o + k] = ln[o + k + 2] + s[k]
        squares = jnp.zeros((C, W2), F32)
        cost = jnp.zeros((C, W2), F32)
        for o in range(0, 4, 2):
            s = sum_lats(dot(k2_ref[...], window(hid_prev, o, F)))
            for k in range(2):
                m = x_prev[o + k + 2] + s[k] + b2
                sides = []
                for side in range(2):
                    i = o + k + 4 * side
                    x = x_ref[i + 2]
                    before = m if side == 0 else halves(m)
                    first = jnp.where(place > 0, mw * (x - before), 0.0)
                    lo = jnp.where(left, first, halves(ln[i + 2]))
                    dep = jnp.where(left & (place == 0), x - bg_ref[i], 0.0)
                    seen = s0_ref[i]
                    if second:
                        seen = seen - alpha_ref[...] * s1_ref[i]
                    g = lo - gh[i] + seen + bw * dep
                    g_ref[i] = g
                    sides.append(g)
                    squares = squares + g * g
                    cost = cost + lo * lo / mw + bw * dep * dep
                if not second:
                    send0[o + k] = jnp.where(even, sides[1], sides[0]).astype(BF16)
                    send1[o + k] = jnp.where(even, sides[0], sides[1]).astype(BF16)
        r = r0_ref[...]
        if second:
            r = r - alpha_ref[:, :1] * r1_ref[...]
        paid = jnp.sum(wt_ref[...] * r * r, axis=1, keepdims=True)
        norm = jnp.sum(jnp.sum(squares, axis=0, keepdims=True), axis=1, keepdims=True)
        paid = 0.5 * (paid + jnp.sum(jnp.sum(cost, axis=0, keepdims=True), axis=1, keepdims=True))
        lane = lax.broadcasted_iota(jnp.int32, (n_all, W2), 1)
        row_ref[...] = jnp.where(lane == 0, norm, jnp.where(lane == 1, paid, 0.0))

    return kernel


def gradient(n_tm, n_all, ins, second):
    edge = ((HALO, C, W2), BF16)
    outs = [((BAND, C, W2), F32), ((n_all, W2), F32)] + ([] if second else [edge, edge])
    scratch = [pltpu.VMEM((12 * 3 * C, W2), BF16), pltpu.VMEM((10 * F, W2), BF16), pltpu.VMEM((12, C, W2), F32)]
    scratch += [pltpu.VMEM((BAND, C, W2), F32), pltpu.VMEM((8 * 3 * C, W2), BF16), pltpu.VMEM((6 * F, W2), BF16)]
    scratch += [pltpu.VMEM((8, C, W2), F32)]
    return call(gradient_kernel(second, n_tm, n_all), ins, outs, scratch, limit=16)


def final_kernel(total):
    def kernel(step_ref, first_ref, sums_ref, x_ref, g_ref, x_out, cost_out, buf, sems):
        alpha = step_from(sums_ref[...], step_ref[...], total)
        copies = []
        for i in range(BAND):
            v = x_ref[i + 2] - alpha * g_ref[i]
            v = jnp.concatenate([v, jnp.zeros((W2 - C, W2), F32)], axis=0).T[:, :C]
            buf[0, i] = v[:LAT]
            buf[1, i] = v[LAT:]
            copies += [pltpu.make_async_copy(buf.at[k, i], x_out.at[k, i], sems.at[k, i]) for k in range(2)]
            copies[-2].start()
            copies[-1].start()
        c0 = jnp.sum(first_ref[...], axis=0, keepdims=True)
        c1 = jnp.sum(sums_ref[...], axis=0, keepdims=True)
        lane = lax.broadcasted_iota(jnp.int32, c0.shape, 1)
        one = jnp.sum(jnp.where(lane == 1, c0, 0.0), axis=1, keepdims=True)
        two = jnp.sum(jnp.where(lane == 1, c1, 0.0), axis=1, keepdims=True)
        cost_out[...] = jnp.where(lane == 0, one, two)[:, :2]
        for copy in copies:
            copy.wait()

    return kernel


def swapped(value, axes, first):
    n = lax.axis_size(axes)
    closed = axes == LON
    pairs = []
    for i in range(first, n, 2):
        j = (i + 1) % n
        if closed or j > i:
            pairs += [(i, j), (j, i)]
    return lax.ppermute(value, axes, pairs)


def exchange(place, band, mine0, mine1):
    got0 = swapped(mine0, LON, 0)
    got1 = swapped(mine1, LON, 1)
    send0, send1 = strips(place, band, mine0, mine1, got0, got1)
    strip0 = swapped(send0, TM, 0)
    strip1 = swapped(send1, TM, 1)
    return got0, got1, strip0, strip1, send0


def per_device(x, background, opening, b1, closing, b2, mw, bw, cell, chan, val, wt, step):
    n_tm = lax.axis_size(TM)
    n_all = n_tm * lax.axis_size(LON)
    total = float(2 * BAND * C * LAT * n_all)
    place = lax.axis_index(TM).astype(jnp.int32)[None]
    band = lax.axis_index(LON).astype(jnp.int32)[None]
    xp, mine0, mine1, place, band, step = pack(place, band, step[None], jnp.swapaxes(x, 2, 3))
    got0, got1, strip0, strip1, _ = exchange(place, band, mine0, mine1)
    o, k2, wia, woa, bias, small, bgp = prepare_weights(
        opening.T, closing, b1, b2, mw, bw, jnp.swapaxes(background, 1, 2)
    )
    nets = (o, k2, bias, small)
    own = (band, xp, got0, got1) + nets
    x0, m0, slope = forward(total, own, False)
    r0, s0, hot, chan, wt = observe_first(cell, chan, val, wt, xp)
    rest = (bgp, wt, woa, wia) + nets
    g0, row, mine0, mine1 = gradient(n_tm, n_all, (place, band, x0, m0, slope, strip0, strip1, r0, s0) + rest, False)
    sums0 = lax.all_to_all(row, TM_LON, 0, 0, tiled=True)
    ggot0, ggot1, gstrip0, gstrip1, sent = exchange(place, band, mine0, mine1)
    later_g0, _ = lax.optimization_barrier((g0, sent))
    x1, m1, slope, alpha = forward(total, (step, sums0, g0, ggot0, ggot1) + own, True)
    r1, s1 = observe_later(chan, wt, hot, later_g0)
    ins = (place, band, x1, m1, slope, strip0, strip1, r0, s0, alpha, gstrip0, gstrip1, r1, s1)
    g1, row = gradient(n_tm, n_all, ins + rest, True)
    sums1 = lax.all_to_all(row, TM_LON, 0, 0, tiled=True)
    x2, costs = call(
        final_kernel(total),
        [step, sums0, sums1, x1, g1],
        [((2, BAND, LAT, C), F32), ((1, 2), F32)],
        [pltpu.VMEM((2, BAND, LAT, C), F32), pltpu.SemaphoreType.DMA((2, BAND))],
        far=1,
    )
    return jnp.swapaxes(x2, 2, 3), costs.reshape(2)


def solution(mesh):
    n_tm, n_lon = mesh.devices.shape
    if (n_tm, n_lon) == (8, 32):
        shape = (4, 2, 2, 8, 2)
    else:
        shape = (n_tm, 1, 1, n_lon // 2, 2)
    split = Mesh(mesh.devices.reshape(shape), TM_LON)
    placed = (
        P(TM, LON, None, None),
        P(LON, None, None),
        P(), P(), P(), P(), P(), P(),
        P(TM, LON), P(TM, LON), P(TM, LON), P(TM, LON),
        P(),
    )
    return jax.shard_map(
        per_device,
        mesh=split,
        in_specs=placed,
        out_specs=(P(TM, LON, None, None), P()),
        check_vma=False,
    )
```
